256 devices in a mesh: frame: 32 (over x_lo, z, core), mod: 8 (over y, x_hi).
Axes of the slice: x: 4 (x_hi: 2, x_lo: 2; x = x_hi * 2 + x_lo), y: 4, z: 8, core: 2. Of those that a mesh axis runs over, the one named last changes fastest.
Arguments:
- frames: bfloat16 [4096, 32768], P('frame', 'mod'), may hold values from 0.2 to 64, as said below
- cycle_label: int32 [32768], P('mod'), may hold values from 0 to 15, as said below
- good_pixel: int32 [32768], P('mod'), may hold values from 0 to 1
Outputs:
- correlation: float32 [16, 4096, 1024], P('mod', 'frame')
The draws below stay inside these ranges and needn't reach their ends.
Inputs may be any that keep to these rules, and one draw needn't show every extreme that they name: `cycle_label`: on every block of 4096 consecutive pixels each of the 16 cycles holds exactly 256 pixels, at least one of them with good_pixel 1. `frames`: positive intensities.
All inputs are finite; a program needn't handle non-finite values.
Results may differ from the reference program's by a relative error of at most 0.0003.
Values may be sent and summed in bfloat16 or wider, within the bound.
A program may use at most 64 MiB of HBM per device.

```python
import math
import jax
import jax.numpy as jnp
from jax import lax

CYCLES = 16
LAG = 1024
FB = 128
PIX_DEV = 4096
FRAMES = 4096
PIXELS = 32768


def pixel_layout(key):
    base_key = jax.random.fold_in(key, 11)
    key_order, key_good = jax.random.split(base_key, 2)
    groups = PIXELS // PIX_DEV
    order_keys = jax.random.split(key_order, groups)
    rank_order = jax.vmap(lambda one_key: jax.random.permutation(one_key, PIX_DEV))(order_keys)
    random_good = (jax.random.randint(key_good, (groups, PIX_DEV), 0, 8, dtype=jnp.int32) > 0).astype(jnp.int32)
    forced = rank_order < CYCLES
    labels = (rank_order % CYCLES).reshape(PIXELS).astype(jnp.int32)
    good_flag = jnp.where(forced, 1, random_good).reshape(PIXELS).astype(jnp.int32)
    return (labels, good_flag)


def draw_cycle_label(key, part):
    return pixel_layout(key)[0]


def draw_good_pixel(key, part):
    return pixel_layout(key)[1]


def draw_frames(key, part):
    key_level, key_pixel, key_speckle = jax.random.split(jax.random.fold_in(key, 5), 3)
    frame_level = jax.random.uniform(key_level, (FRAMES, 1), jnp.float32, 0.0, math.log(4.0))
    pixel_gain = jax.random.uniform(key_pixel, (1, PIXELS), jnp.float32, 0.0, math.log(4.0))
    speckle = jnp.exp(jax.random.uniform(key_speckle, (FRAMES, PIXELS), jnp.float32, math.log(0.25), math.log(4.0)))
    return (jnp.exp(frame_level) * jnp.exp(pixel_gain) * speckle).astype(jnp.bfloat16)


def setup_inputs(seed: int = 0) -> dict:
    key_list = jax.random.split(jax.random.key(seed), 4)
    frames = draw_frames(jax.random.fold_in(key_list[3], 71), 0)
    cycle_label = draw_cycle_label(jax.random.fold_in(key_list[3], 71), 0)
    good_pixel = draw_good_pixel(jax.random.fold_in(key_list[3], 71), 0)
    return dict(frames=frames, cycle_label=cycle_label, good_pixel=good_pixel)


def reference(frames, cycle_label, good_pixel):
    cycle_ids = jnp.arange(CYCLES, dtype=jnp.int32)
    weights = jnp.where(cycle_label[:, None] == cycle_ids[None, :], good_pixel[:, None], 0).astype(jnp.bfloat16)
    cycle_counts = jnp.sum(weights.astype(jnp.float32), axis=0)
    cycle_sums = jnp.dot(frames, weights, preferred_element_type=jnp.float32)
    intensity = frames.astype(jnp.float32)
    weight_rows = weights.astype(jnp.float32).T
    padded = jnp.concatenate([intensity, jnp.zeros((LAG, intensity.shape[1]), jnp.float32)], axis=0)
    padded_sums = jnp.concatenate([cycle_sums, jnp.zeros((LAG, CYCLES), jnp.float32)], axis=0)
    window_width = FB + LAG

    def one_block(block_index):
        first_row = (block_index * FB).astype(jnp.int32)
        block_rows = lax.dynamic_slice_in_dim(intensity, first_row, FB, 0)
        window = lax.dynamic_slice_in_dim(padded, first_row, window_width, 0)
        weighted = block_rows[None, :, :] * weight_rows[:, None, :]
        gram_tile = jnp.einsum("rfp,gp->rfg", weighted, window, precision=lax.Precision.HIGHEST)
        later_sums = lax.dynamic_slice_in_dim(padded_sums, first_row, window_width, 0).T
        earlier = later_sums[:, :FB]
        frame_at = first_row + jnp.arange(window_width, dtype=jnp.int32)
        in_range = frame_at < FRAMES
        safe_sums = jnp.where(in_range[None, :], later_sums, 1.0)
        normalized = gram_tile * cycle_counts[:, None, None] / (earlier[:, :, None] * safe_sums[:, None, :])
        normalized = jnp.where(in_range[None, None, :], normalized, 0.0)
        flattened = jnp.pad(normalized.reshape(CYCLES, FB * window_width), ((0, 0), (0, FB)))
        return flattened.reshape(CYCLES, FB, window_width + 1)[:, :, :LAG]

    blocks = lax.map(one_block, jnp.arange(FRAMES // FB, dtype=jnp.int32))
    return blocks.transpose(1, 0, 2, 3).reshape(CYCLES, FRAMES, LAG)
```

```python
import functools

import jax
import jax.numpy as jnp
from jax import lax
from jax.experimental import pallas as pl
from jax.experimental.pallas import tpu as pltpu
from jax.sharding import PartitionSpec as P

CYCLES = 16
LAG = 1024
MESH = pl.DeviceIdType.MESH
NT = (((1,), (1,)), ((), ()))


def nt_dot(a, b):
    return lax.dot_general(a, b, NT, preferred_element_type=jnp.float32)


def arrange_kernel(cycles, per_cycle, frames_ref, label_ref, good_ref, x_ref, count_ref, rank_ref):
    q = pl.program_id(0)
    rows, lanes = label_ref.shape

    @pl.when(q == 0)
    def _():
        label = label_ref[...]
        member = jnp.concatenate(
            [jnp.where(label == c, 1.0, 0.0) for c in range(cycles)], axis=0
        ).astype(jnp.bfloat16)
        before = lax.broadcasted_iota(jnp.int32, (lanes, lanes), 0)
        at = lax.broadcasted_iota(jnp.int32, (lanes, lanes), 1)
        upper = jnp.where(before < at, 1.0, 0.0).astype(jnp.bfloat16)
        in_row = jnp.dot(member, upper, preferred_element_type=jnp.float32)
        totals = jnp.dot(
            member, jnp.ones((lanes, lanes), jnp.bfloat16), preferred_element_type=jnp.float32
        ).astype(jnp.bfloat16)
        size = cycles * rows
        here = lax.broadcasted_iota(jnp.int32, (size, size), 0)
        there = lax.broadcasted_iota(jnp.int32, (size, size), 1)
        earlier = (here // rows == there // rows) & (there < here)
        above = jnp.dot(
            jnp.where(earlier, 1.0, 0.0).astype(jnp.bfloat16),
            totals,
            preferred_element_type=jnp.float32,
        )
        ranks = (in_row + above) * member.astype(jnp.float32)
        total = ranks[:rows]
        for c in range(1, cycles):
            total = total + ranks[c * rows : (c + 1) * rows]
        rank_ref[...] = jnp.where(good_ref[...] > 0, total, -1.0)

    rank = jnp.where(label_ref[...] == q, rank_ref[...], -1.0)
    place = lax.broadcasted_iota(jnp.int32, (per_cycle, lanes), 0).astype(jnp.float32)
    acc = None
    step = 2
    for r in range(0, rows, step):
        hot = jnp.concatenate(
            [
                jnp.where(place == rank[r + i : r + i + 1, :], 1.0, 0.0).astype(jnp.bfloat16)
                for i in range(step)
            ],
            axis=1,
        )
        term = nt_dot(frames_ref[:, r * lanes : (r + step) * lanes], hot)
        acc = term if acc is None else acc + term
    x_ref[0, 0] = acc.astype(jnp.bfloat16)
    count = jnp.sum(jnp.where(rank >= 0.0, 1.0, 0.0))
    mine = lax.broadcasted_iota(jnp.int32, count_ref.shape[1:], 0) == q % 2
    count_ref[0] = jnp.where(mine, count, count_ref[0])


def arrange(frames, label, good, per_cycle):
    rows, pixels = frames.shape
    lanes = 128
    packed = (pixels // lanes, lanes)
    cycles = pixels // per_cycle
    return pl.pallas_call(
        functools.partial(arrange_kernel, cycles, per_cycle),
        grid=(cycles,),
        in_specs=[
            pl.BlockSpec((rows, pixels), lambda q: (0, 0)),
            pl.BlockSpec(packed, lambda q: (0, 0)),
            pl.BlockSpec(packed, lambda q: (0, 0)),
        ],
        out_specs=[
            pl.BlockSpec((1, 1, rows, per_cycle), lambda q: (q % 2, q // 2, 0, 0)),
            pl.BlockSpec((1, 8, lanes), lambda q: (q // 2, 0, 0)),
        ],
        out_shape=[
            jax.ShapeDtypeStruct((2, cycles // 2, rows, per_cycle), jnp.bfloat16),
            jax.ShapeDtypeStruct((cycles // 2, 8, lanes), jnp.float32),
        ],
        scratch_shapes=[pltpu.VMEM(packed, jnp.float32)],
    )(frames, label.reshape(packed), good.reshape(packed))


def exchange_kernel(
    frame_count, mod_count, x_ref, c_ref, out_ref,
    held, counts, tiles, far, recv_sem, send_sem, count_send, count_recv, far_send, far_recv,
):
    f = lax.axis_index("frame")
    m = lax.axis_index("mod")
    core = f % 2
    chip = f // 2
    chips = frame_count // 2
    y_count = mod_count // 2
    y, x = m // 2, m % 2
    partner = f + 1 - 2 * core
    steps = 2 * mod_count

    has_up1, has_up2 = chip + 1 < chips, chip + 2 < chips
    has_dn1, has_dn2 = chip >= 1, chip >= 2

    own, down1, down2, up1, up2 = 4 + core, 6 + core, 8 + core, 2 + core, core
    other_down1, other_down2, other_own = 7 - core, 9 - core, 5 - core

    def peer(o, sign):
        dy, dx = o // 2, o % 2
        return ((y + sign * dy + y_count) % y_count) * 2 + (x + dx) % 2

    barrier = pltpu.get_barrier_semaphore()

    def greet(cond, fr, mo):
        @pl.when(cond)
        def _():
            pl.semaphore_signal(barrier, inc=1, device_id=(fr, mo), device_id_type=MESH)

    for o in range(1, mod_count):
        pl.semaphore_signal(barrier, inc=1, device_id=(f, peer(o, 1)), device_id_type=MESH)
    pl.semaphore_signal(barrier, inc=1, device_id=(partner, m), device_id_type=MESH)
    greet(has_up1, f + 2, m)
    greet(has_up2, f + 4, m)
    greet(has_dn1, f - 2, m)
    greet(has_dn2, f - 4, m)
    arrivals = mod_count
    for cond in (has_up1, has_up2, has_dn1, has_dn2):
        arrivals = arrivals + jnp.where(cond, 1, 0)
    pl.semaphore_wait(barrier, arrivals)

    def remote(src, dst, send, recv, fr, mo):
        return pltpu.make_async_remote_copy(
            src_ref=src, dst_ref=dst, send_sem=send, recv_sem=recv,
            device_id=(fr, mo), device_id_type=MESH,
        )

    def forward(from_slot, to_slot, k, lane, fr):
        remote(
            held.at[from_slot, k], held.at[to_slot, k], send_sem.at[lane],
            recv_sem.at[to_slot, k], fr, m,
        ).start()

    def arrived(slot, k):
        pltpu.make_async_copy(held.at[slot, k], held.at[slot, k], recv_sem.at[slot, k]).wait()

    for cyc in range(2):
        pltpu.make_async_copy(
            x_ref.at[cyc, m], held.at[own, cyc * mod_count], recv_sem.at[own, cyc * mod_count]
        ).start()
    pltpu.make_async_copy(c_ref.at[m], counts.at[0], count_recv.at[0]).start()

    def spread(cyc):
        @pl.loop(1, mod_count)
        def _(o):
            to = peer(o, -1)
            k = cyc * mod_count + o
            remote(
                x_ref.at[cyc, to], held.at[own, k], send_sem.at[0], recv_sem.at[own, k], f, to
            ).start()

    spread(0)
    spread(1)
    for o in range(1, mod_count):
        to = peer(o, -1)
        remote(c_ref.at[to], counts.at[o], count_send.at[o], count_recv.at[o], f, to).start()

    def step(k):
        @pl.when(k < steps)
        def _():
            arrived(own, k)

            @pl.when(has_dn1)
            def _():
                forward(own, down1, k, 1, f - 2)

            @pl.when(has_up1)
            def _():
                forward(own, up1, k, 2, f + 2)

            forward(own, own, k, 3, partner)

        k1 = k - 1

        @pl.when((k1 >= 0) & (k1 < steps))
        def _():
            @pl.when(has_up1)
            def _():
                arrived(down1, k1)

                @pl.when(has_dn1)
                def _():
                    forward(down1, down2, k1, 4, f - 2)

                forward(down1, down1, k1, 5, partner)

            @pl.when(has_dn1)
            def _():
                arrived(up1, k1)

                @pl.when(has_up1)
                def _():
                    forward(up1, up2, k1, 6, f + 2)

        k2 = k - 2

        @pl.when((k2 >= 0) & (k2 < steps) & has_up2)
        def _():
            arrived(down2, k2)
            forward(down2, down2, k2, 7, partner)

    def product(lhs_slot, rhs_slot, cyc):
        total, later, earlier = None, None, None
        ones = jnp.ones((128, 256), jnp.bfloat16)
        for o in range(mod_count):
            k = cyc * mod_count + o
            lhs = held[lhs_slot, k]
            rhs = held[rhs_slot : rhs_slot + 2, k].reshape(256, 256)
            a, b, c = nt_dot(lhs, rhs), nt_dot(ones[:8], rhs), nt_dot(lhs, ones)
            if total is None:
                total, later, earlier = a, b, c
            else:
                total, later, earlier = total + a, later + b, earlier + c
        count = counts[0]
        for o in range(1, mod_count):
            count = count + counts[o]
        count = count[cyc : cyc + 1]
        return [
            total[:, i * 128 : i * 128 + 128] * count
            / (earlier * later[0:1, i * 128 : i * 128 + 128])
            for i in range(2)
        ]

    def far_copy(kind, cyc):
        distance = 2 if kind == 0 else 4
        return remote(
            far.at[kind, cyc], tiles.at[cyc, pl.ds(6 + 2 * kind, 2)],
            far_send.at[kind, cyc], far_recv.at[kind, cyc], f - distance, m,
        )

    def compute(cyc):
        @pl.loop(0, mod_count)
        def _(o):
            k = cyc * mod_count + o
            arrived(other_own, k)

            @pl.when(has_up1)
            def _():
                arrived(other_down1, k)

            @pl.when(has_up2)
            def _():
                arrived(other_down2, k)

            @pl.when(has_dn2)
            def _():
                arrived(up2, k)

        for kind, slot, cond in ((1, up2, has_dn2 & has_up2), (0, up1, has_dn1 & has_up2)):
            @pl.when(cond)
            def _():
                for i, tile in enumerate(product(slot, 8, cyc)):
                    far[kind, cyc, i] = tile
                far_copy(kind, cyc).start()

        for piece, cond in ((0, None), (1, has_up1), (2, has_up2)):
            def fill(piece=piece):
                for i, tile in enumerate(product(own, 4 + 2 * piece, cyc)):
                    tiles[cyc, 2 * piece + i] = tile

            if cond is None:
                fill()
            else:
                pl.when(cond)(fill)

                @pl.when(jnp.logical_not(cond))
                def _():
                    tiles[cyc, 2 * piece : 2 * piece + 2] = jnp.zeros((2, 128, 128), jnp.float32)

    def finish(cyc):
        for kind, distance in ((0, 3), (1, 4)):
            @pl.when(chip + distance < chips)
            def _():
                far_copy(kind, cyc).wait_recv()

            @pl.when(chip + distance >= chips)
            def _():
                tiles[cyc, 6 + 2 * kind : 8 + 2 * kind] = jnp.zeros((2, 128, 128), jnp.float32)

        row = lax.broadcasted_iota(jnp.int32, (128, 128), 0)
        lane = lax.broadcasted_iota(jnp.int32, (128, 128), 1)
        inside = lane + row < 128

        def turned(j):
            tile = tiles[cyc, core + j]
            for bit in (1, 2, 4):
                tile = jnp.where(row // bit % 2 == 1, pltpu.roll(tile, 128 - bit, 1), tile)
            return jnp.concatenate(
                [tile[:8]] + [pltpu.roll(tile[r : r + 8], 128 - r, 1) for r in range(8, 128, 8)], axis=0
            )

        now = turned(0)
        for j in range(LAG // 128):
            later = turned(j + 1)
            out_ref[cyc, :, j * 128 : j * 128 + 128] = jnp.where(inside, now, later)
            now = later

    middle = mod_count + 4

    @pl.loop(0, middle)
    def _(k):
        step(k)

    for o in range(mod_count):
        pltpu.make_async_copy(counts.at[o], counts.at[o], count_recv.at[o]).wait()
    compute(0)

    @pl.loop(middle, steps + 2)
    def _(k):
        step(k)

    finish(0)
    compute(1)
    finish(1)

    def sent(lane, slot):
        pltpu.make_async_copy(held.at[slot], held.at[slot], send_sem.at[lane]).wait()

    for cyc in range(2):
        pltpu.make_async_copy(
            held.at[own, pl.ds(cyc * mod_count + 1, mod_count - 1)],
            held.at[own, pl.ds(cyc * mod_count + 1, mod_count - 1)],
            send_sem.at[0],
        ).wait()
    for o in range(1, mod_count):
        pltpu.make_async_copy(counts.at[o], counts.at[o], count_send.at[o]).wait()
    for lane, slot, cond in (
        (1, own, has_dn1), (2, own, has_up1), (3, own, None), (4, down1, has_up1 & has_dn1),
        (5, down1, has_up1), (6, up1, has_up1 & has_dn1), (7, down2, has_up2),
    ):
        if cond is None:
            sent(lane, slot)
        else:
            pl.when(cond)(functools.partial(sent, lane, slot))
    for cyc in range(2):
        for kind, cond in ((1, has_dn2 & has_up2), (0, has_dn1 & has_up2)):
            @pl.when(cond)
            def _():
                far_copy(kind, cyc).wait_send()


def exchange(x, c, frame_count, mod_count):
    rows, per_cycle = x.shape[2:]
    steps = 2 * mod_count
    return pl.pallas_call(
        functools.partial(exchange_kernel, frame_count, mod_count),
        out_shape=jax.ShapeDtypeStruct((2, rows, LAG), jnp.float32),
        in_specs=[pl.BlockSpec(memory_space=pltpu.VMEM)] * 2,
        out_specs=pl.BlockSpec(memory_space=pltpu.VMEM),
        scratch_shapes=[
            pltpu.VMEM((10, steps, rows, per_cycle), jnp.bfloat16),
            pltpu.VMEM((mod_count, 8, 128), jnp.float32),
            pltpu.VMEM((2, 10, 128, 128), jnp.float32),
            pltpu.VMEM((2, 2, 2, 128, 128), jnp.float32),
            pltpu.SemaphoreType.DMA((10, steps)),
            pltpu.SemaphoreType.DMA((8,)),
            pltpu.SemaphoreType.DMA((mod_count,)),
            pltpu.SemaphoreType.DMA((mod_count,)),
            pltpu.SemaphoreType.DMA((2, 2)),
            pltpu.SemaphoreType.DMA((2, 2)),
        ],
        compiler_params=pltpu.CompilerParams(
            collective_id=0, has_side_effects=True, vmem_limit_bytes=32 * 1024 * 1024
        ),
    )(x, c)


def shards(frames, cycle_label, good_pixel):
    mod_count = lax.axis_size("mod")
    per_cycle = frames.shape[1] // (2 * mod_count)
    x, c = arrange(frames, cycle_label, good_pixel, per_cycle)
    return exchange(x, c, lax.axis_size("frame"), mod_count)


def solution(mesh):
    placed = (P("frame", "mod"), P("mod"), P("mod"))
    return jax.shard_map(
        shards, mesh=mesh, in_specs=placed, out_specs=P("mod", "frame", None), check_vma=False
    )
```

```python
import functools

import jax
import jax.numpy as jnp
from jax import lax
from jax.experimental import pallas as pl
from jax.experimental.pallas import tpu as pltpu
from jax.sharding import PartitionSpec as P

CYCLES = 16
LAG = 1024
MESH = pl.DeviceIdType.MESH
NT = (((1,), (1,)), ((), ()))
RELAY_LAG = 3
SHARE_LAG = 6
FIRST_GRAM = 7


def nt_dot(a, b):
    return lax.dot_general(a, b, NT, preferred_element_type=jnp.float32)


def rank_pixels(label_ref, good_ref, place, partial, cycles, per_cycle):
    rows, lanes = label_ref.shape
    label = label_ref[...]
    good = good_ref[...] > 0
    member = jnp.concatenate([jnp.where(label == c, 1.0, 0.0) for c in range(cycles)], axis=0)
    before = lax.broadcasted_iota(jnp.int32, (lanes, lanes), 0)
    at = lax.broadcasted_iota(jnp.int32, (lanes, lanes), 1)
    upper = jnp.where(before < at, 1.0, 0.0).astype(jnp.bfloat16)
    ones = jnp.ones((lanes, lanes), jnp.bfloat16)
    packed = member.astype(jnp.bfloat16)
    in_row = jnp.dot(packed, upper, preferred_element_type=jnp.float32)
    totals = jnp.dot(packed, ones, preferred_element_type=jnp.float32).astype(jnp.bfloat16)
    size = cycles * rows
    here = lax.broadcasted_iota(jnp.int32, (size, size), 0)
    there = lax.broadcasted_iota(jnp.int32, (size, size), 1)
    earlier = jnp.where((here // rows == there // rows) & (there < here), 1.0, 0.0)
    above = jnp.dot(earlier.astype(jnp.bfloat16), totals, preferred_element_type=jnp.float32)
    ranks = (in_row + above) * member
    usable = jnp.where(good, 1.0, 0.0)
    partial[...] = jnp.zeros_like(partial)
    total = None
    for c in range(cycles):
        mine = slice(c * rows, (c + 1) * rows)
        total = ranks[mine] if total is None else total + ranks[mine]
        per_row = jnp.sum(member[mine] * usable, axis=0, keepdims=True)
        partial[c // 2, c % 2 : c % 2 + 1, :] = jnp.broadcast_to(
            jnp.sum(per_row, axis=1, keepdims=True), (1, lanes)
        )
    where = jnp.where(good, total + label.astype(jnp.float32) * per_cycle, -1.0)
    for r in range(rows):
        place[r * lanes : (r + 1) * lanes, :] = jnp.broadcast_to(where[r : r + 1], (lanes, lanes)).T


def kernel(
    frame_count, mod_count, frames_hbm, label_hbm, good_hbm, out_hbm,
    frames, label, good, place, partial, packed, held, counts, tiles, far, out,
    in_sem, out_sem, recv_sem, send_sem, count_send, count_recv, far_send, far_recv,
):
    f = lax.axis_index("frame")
    m = lax.axis_index("mod")
    core = f % 2
    chip = f // 2
    chips = frame_count // 2
    y_count = mod_count // 2
    y, x = m // 2, m % 2
    partner = f + 1 - 2 * core
    steps = 2 * mod_count
    cycles = 2 * mod_count
    rows, per_cycle = packed.shape[1:]

    has_up1, has_up2 = chip + 1 < chips, chip + 2 < chips
    has_dn1, has_dn2 = chip >= 1, chip >= 2

    own, down1, down2, up1, up2 = 4 + core, 6 + core, 8 + core, 2 + core, core
    other_down1, other_down2, other_own = 7 - core, 9 - core, 5 - core

    loads = [
        pltpu.make_async_copy(src, dst, in_sem.at[i])
        for i, (src, dst) in enumerate(
            ((label_hbm, label), (good_hbm, good), (frames_hbm, frames))
        )
    ]
    for load in loads:
        load.start()

    def peer(o, sign):
        dy, dx = o // 2, o % 2
        return ((y + sign * dy + y_count) % y_count) * 2 + (x + dx) % 2

    barrier = pltpu.get_barrier_semaphore()

    def greet(cond, fr, mo):
        @pl.when(cond)
        def _():
            pl.semaphore_signal(barrier, inc=1, device_id=(fr, mo), device_id_type=MESH)

    for o in range(1, mod_count):
        pl.semaphore_signal(barrier, inc=1, device_id=(f, peer(o, 1)), device_id_type=MESH)
    pl.semaphore_signal(barrier, inc=1, device_id=(partner, m), device_id_type=MESH)
    greet(has_up1, f + 2, m)
    greet(has_up2, f + 4, m)
    greet(has_dn1, f - 2, m)
    greet(has_dn2, f - 4, m)
    arrivals = mod_count
    for cond in (has_up1, has_up2, has_dn1, has_dn2):
        arrivals = arrivals + jnp.where(cond, 1, 0)

    loads[0].wait()
    loads[1].wait()
    rank_pixels(label, good, place, partial, cycles, per_cycle)
    loads[2].wait()
    pl.semaphore_wait(barrier, arrivals)

    def remote(src, dst, send, recv, fr, mo):
        return pltpu.make_async_remote_copy(
            src_ref=src, dst_ref=dst, send_sem=send, recv_sem=recv,
            device_id=(fr, mo), device_id_type=MESH,
        )

    def forward(from_slot, to_slot, k, lane, fr):
        remote(
            held.at[from_slot, k], held.at[to_slot, k], send_sem.at[lane],
            recv_sem.at[to_slot, k], fr, m,
        ).start()

    def arrived(slot, k):
        pltpu.make_async_copy(held.at[slot, k], held.at[slot, k], recv_sem.at[slot, k]).wait()

    def arrange(k):
        cyc, o = k // mod_count, k % mod_count
        cycle = 2 * peer(o, -1) + cyc
        lane = lax.broadcasted_iota(jnp.int32, (256, 128), 1) + cycle * per_cycle
        wanted = [(lane + h * 128).astype(jnp.float32) for h in range(per_cycle // 128)]
        total = None
        for r in range(0, frames.shape[1], 256):
            spot = place[r : r + 256, :]
            hot = jnp.concatenate(
                [jnp.where(spot == w, 1.0, 0.0).astype(jnp.bfloat16) for w in wanted], axis=1
            )
            term = jnp.dot(frames[:, r : r + 256], hot, preferred_element_type=jnp.float32)
            total = term if total is None else total + term
        packed[k] = total.astype(jnp.bfloat16)

    def launch(k):
        o = k % mod_count

        @pl.when(o == 0)
        def _():
            pltpu.make_async_copy(packed.at[k], held.at[own, k], recv_sem.at[own, k]).start()

        @pl.when(o > 0)
        def _():
            remote(
                packed.at[k], held.at[own, k], send_sem.at[0], recv_sem.at[own, k], f, peer(o, -1)
            ).start()

    def own_stage(k):
        arrived(own, k)

        @pl.when(has_dn1)
        def _():
            forward(own, down1, k, 1, f - 2)

        @pl.when(has_up1)
        def _():
            forward(own, up1, k, 2, f + 2)

        forward(own, own, k, 3, partner)

    def relay_stage(k):
        @pl.when(has_up1)
        def _():
            arrived(down1, k)

            @pl.when(has_dn1)
            def _():
                forward(down1, down2, k, 4, f - 2)

            forward(down1, down1, k, 5, partner)

        @pl.when(has_dn1)
        def _():
            arrived(up1, k)

            @pl.when(has_up1)
            def _():
                forward(up1, up2, k, 6, f + 2)

    def share_stage(k):
        @pl.when(has_up2)
        def _():
            arrived(down2, k)
            forward(down2, down2, k, 7, partner)

    @pl.loop(0, mod_count + 1)
    def _(o):
        @pl.when(o < mod_count)
        def _():
            arrange(o)

        @pl.when(o >= 1)
        def _():
            launch(o - 1)

        @pl.when(o == 2)
        def _():
            own_stage(0)

    for o in range(mod_count):
        to = peer(o, -1)
        if o == 0:
            pltpu.make_async_copy(partial.at[to], counts.at[o], count_recv.at[o]).start()
        else:
            remote(partial.at[to], counts.at[o], count_send.at[o], count_recv.at[o], f, to).start()

    def step(k):
        @pl.when((k >= 1) & (k < steps))
        def _():
            own_stage(k)

        @pl.when(k < mod_count)
        def _():
            arrange(mod_count + k)

        @pl.when((k >= 1) & (k <= mod_count))
        def _():
            launch(mod_count + k - 1)

        @pl.when((k >= RELAY_LAG) & (k < steps + RELAY_LAG))
        def _():
            relay_stage(k - RELAY_LAG)

        @pl.when((k >= SHARE_LAG) & (k < steps + SHARE_LAG))
        def _():
            share_stage(k - SHARE_LAG)

    def far3_copy(cyc):
        return remote(
            far.at[cyc, pl.ds(0, 2)], tiles.at[cyc, pl.ds(6, 2)],
            far_send.at[cyc, 0], far_recv.at[cyc, 0], f - 2, m,
        )

    def far4_copy(cyc, i):
        return remote(
            far.at[cyc, 2 + i], tiles.at[cyc, 8 + i],
            far_send.at[cyc, 1 + i], far_recv.at[cyc, 1 + i], f - 4, m,
        )

    sends3, sends4 = has_dn1 & has_up2, has_dn2 & has_up2

    def compute(cyc):
        @pl.loop(0, mod_count)
        def _(o):
            k = cyc * mod_count + o
            arrived(other_own, k)

            @pl.when(has_up1)
            def _():
                arrived(other_down1, k)

            @pl.when(has_up2)
            def _():
                arrived(other_down2, k)

            @pl.when(has_dn2)
            def _():
                arrived(up2, k)

        count = counts[0]
        for o in range(1, mod_count):
            count = count + counts[o]
        count = count[cyc : cyc + 1]
        ones = jnp.ones((16, per_cycle), jnp.bfloat16)

        def products(lhs_slots, rhs_slot):
            total = None
            for o in range(mod_count):
                k = cyc * mod_count + o
                lhs = jnp.concatenate([held[s, k] for s in lhs_slots] + [ones], axis=0)
                rhs = held[rhs_slot : rhs_slot + 2, k].reshape(2 * rows, per_cycle)
                term = nt_dot(lhs, rhs)
                total = term if total is None else total + term
            return total

        def row_sums(slot):
            total = None
            for o in range(mod_count):
                block = held[slot, cyc * mod_count + o].astype(jnp.float32)
                total = block if total is None else total + block
            return jnp.sum(total, axis=1, keepdims=True)

        def tile(total, i, earlier, later, half):
            span = slice(half * 128, half * 128 + 128)
            return total[i * 128 : i * 128 + 128, span] * count / (earlier * later[:, span])

        mine = row_sums(own)

        @pl.when(has_up2)
        def _():
            total = products((up1, up2, own), 8)
            later = total[3 * rows : 3 * rows + 1]
            first, second = row_sums(up1), row_sums(up2)
            for half in range(2):
                far[cyc, half] = tile(total, 0, first, later, half)
                far[cyc, 2 + half] = tile(total, 1, second, later, half)
            for half in range(2):
                tiles[cyc, 4 + half] = tile(total, 2, mine, later, half)

        @pl.when(sends4)
        def _():
            far4_copy(cyc, 0).start()

            @pl.when(core == 1)
            def _():
                far4_copy(cyc, 1).start()

        @pl.when(sends3)
        def _():
            far3_copy(cyc).start()

        @pl.when(jnp.logical_not(has_up2))
        def _():
            tiles[cyc, 4:6] = jnp.zeros((2, 128, 128), jnp.float32)

        def near(rhs_slot):
            total = products((own,), rhs_slot)
            for half in range(2):
                tiles[cyc, rhs_slot - 4 + half] = tile(
                    total, 0, mine, total[rows : rows + 1], half
                )

        near(4)

        @pl.when(has_up1)
        def _():
            near(6)

        @pl.when(jnp.logical_not(has_up1))
        def _():
            tiles[cyc, 2:4] = jnp.zeros((2, 128, 128), jnp.float32)

    def out_copy(cyc):
        return pltpu.make_async_copy(out.at[cyc], out_hbm.at[cyc], out_sem.at[cyc])

    def finish(cyc):
        @pl.when(chip + 3 < chips)
        def _():
            far3_copy(cyc).wait_recv()

        @pl.when(chip + 3 >= chips)
        def _():
            tiles[cyc, 6:8] = jnp.zeros((2, 128, 128), jnp.float32)

        @pl.when(chip + 4 < chips)
        def _():
            far4_copy(cyc, 0).wait_recv()

            @pl.when(core == 1)
            def _():
                far4_copy(cyc, 1).wait_recv()

        @pl.when(chip + 4 >= chips)
        def _():
            tiles[cyc, 8:10] = jnp.zeros((2, 128, 128), jnp.float32)

        row = lax.broadcasted_iota(jnp.int32, (128, 128), 0)
        lane = lax.broadcasted_iota(jnp.int32, (128, 128), 1)
        inside = lane + row < 128

        def turned(j):
            piece = tiles[cyc, core + j]
            for bit in (1, 2, 4):
                piece = jnp.where(row // bit % 2 == 1, pltpu.roll(piece, 128 - bit, 1), piece)
            return jnp.concatenate(
                [piece[:8]] + [pltpu.roll(piece[r : r + 8], 128 - r, 1) for r in range(8, 128, 8)],
                axis=0,
            )

        now = turned(0)
        for j in range(LAG // 128):
            later = turned(j + 1)
            out[cyc, :, j * 128 : j * 128 + 128] = jnp.where(inside, now, later)
            now = later
        out_copy(cyc).start()

    middle = mod_count + FIRST_GRAM

    @pl.loop(0, middle)
    def _(k):
        step(k)

    for o in range(mod_count):
        pltpu.make_async_copy(counts.at[o], counts.at[o], count_recv.at[o]).wait()
    compute(0)

    @pl.loop(middle, steps + SHARE_LAG)
    def _(k):
        step(k)

    finish(0)
    compute(1)
    finish(1)

    def sent(lane, slot):
        pltpu.make_async_copy(held.at[slot], held.at[slot], send_sem.at[lane]).wait()

    for cyc in range(2):
        part = held.at[own, pl.ds(cyc * mod_count + 1, mod_count - 1)]
        pltpu.make_async_copy(part, part, send_sem.at[0]).wait()
    for o in range(1, mod_count):
        pltpu.make_async_copy(counts.at[o], counts.at[o], count_send.at[o]).wait()
    for lane, slot, cond in (
        (1, own, has_dn1), (2, own, has_up1), (3, own, None), (4, down1, has_up1 & has_dn1),
        (5, down1, has_up1), (6, up1, has_up1 & has_dn1), (7, down2, has_up2),
    ):
        if cond is None:
            sent(lane, slot)
        else:
            pl.when(cond)(functools.partial(sent, lane, slot))
    for cyc in range(2):
        @pl.when(sends3)
        def _():
            far3_copy(cyc).wait_send()

        @pl.when(sends4)
        def _():
            far4_copy(cyc, 0).wait_send()

            @pl.when(core == 1)
            def _():
                far4_copy(cyc, 1).wait_send()
        out_copy(cyc).wait()


def shards(frames, cycle_label, good_pixel):
    frame_count, mod_count = lax.axis_size("frame"), lax.axis_size("mod")
    rows, pixels = frames.shape
    steps = 2 * mod_count
    per_cycle = pixels // steps
    small = (pixels // 128, 128)
    return pl.pallas_call(
        functools.partial(kernel, frame_count, mod_count),
        out_shape=jax.ShapeDtypeStruct((2, rows, LAG), jnp.float32),
        in_specs=[pl.BlockSpec(memory_space=pl.ANY)] * 3,
        out_specs=pl.BlockSpec(memory_space=pl.ANY),
        scratch_shapes=[
            pltpu.VMEM((rows, pixels), jnp.bfloat16),
            pltpu.VMEM(small, jnp.int32),
            pltpu.VMEM(small, jnp.int32),
            pltpu.VMEM((pixels, 128), jnp.float32),
            pltpu.VMEM((mod_count, 8, 128), jnp.float32),
            pltpu.VMEM((steps, rows, per_cycle), jnp.bfloat16),
            pltpu.VMEM((10, steps, rows, per_cycle), jnp.bfloat16),
            pltpu.VMEM((mod_count, 8, 128), jnp.float32),
            pltpu.VMEM((2, 10, 128, 128), jnp.float32),
            pltpu.VMEM((2, 4, 128, 128), jnp.float32),
            pltpu.VMEM((2, rows, LAG), jnp.float32),
            pltpu.SemaphoreType.DMA((3,)),
            pltpu.SemaphoreType.DMA((2,)),
            pltpu.SemaphoreType.DMA((10, steps)),
            pltpu.SemaphoreType.DMA((8,)),
            pltpu.SemaphoreType.DMA((mod_count,)),
            pltpu.SemaphoreType.DMA((mod_count,)),
            pltpu.SemaphoreType.DMA((2, 3)),
            pltpu.SemaphoreType.DMA((2, 3)),
        ],
        compiler_params=pltpu.CompilerParams(
            collective_id=0, has_side_effects=True, vmem_limit_bytes=60 * 1024 * 1024
        ),
    )(frames, cycle_label.reshape(small), good_pixel.reshape(small))


def solution(mesh):
    placed = (P("frame", "mod"), P("mod"), P("mod"))
    return jax.shard_map(
        shards, mesh=mesh, in_specs=placed, out_specs=P("mod", "frame", None), check_vma=False
    )
```

```python
import functools

import jax
import jax.numpy as jnp
from jax import lax
from jax.experimental import pallas as pl
from jax.experimental.pallas import tpu as pltpu
from jax.sharding import PartitionSpec as P

CYCLES = 16
LAG = 1024
MESH = pl.DeviceIdType.MESH
NT = (((1,), (1,)), ((), ()))


def nt_dot(a, b):
    return lax.dot_general(a, b, NT, preferred_element_type=jnp.float32)


def rank_pixels(label_ref, good_ref, place, partial, cycles, per_cycle):
    rows, lanes = label_ref.shape
    label = label_ref[...]
    good = good_ref[...] > 0
    member = jnp.concatenate([jnp.where(label == c, 1.0, 0.0) for c in range(cycles)], axis=0)
    before = lax.broadcasted_iota(jnp.int32, (lanes, lanes), 0)
    at = lax.broadcasted_iota(jnp.int32, (lanes, lanes), 1)
    upper = jnp.where(before < at, 1.0, 0.0).astype(jnp.bfloat16)
    ones = jnp.ones((lanes, lanes), jnp.bfloat16)
    packed = member.astype(jnp.bfloat16)
    in_row = jnp.dot(packed, upper, preferred_element_type=jnp.float32)
    totals = jnp.dot(packed, ones, preferred_element_type=jnp.float32).astype(jnp.bfloat16)
    size = cycles * rows
    here = lax.broadcasted_iota(jnp.int32, (size, size), 0)
    there = lax.broadcasted_iota(jnp.int32, (size, size), 1)
    earlier = jnp.where((here // rows == there // rows) & (there < here), 1.0, 0.0)
    above = jnp.dot(earlier.astype(jnp.bfloat16), totals, preferred_element_type=jnp.float32)
    ranks = (in_row + above) * member
    usable = jnp.where(good, 1.0, 0.0)
    partial[...] = jnp.zeros_like(partial)
    total = None
    for c in range(cycles):
        mine = slice(c * rows, (c + 1) * rows)
        total = ranks[mine] if total is None else total + ranks[mine]
        per_row = jnp.sum(member[mine] * usable, axis=0, keepdims=True)
        partial[c // 2, c % 2 : c % 2 + 1, :] = jnp.broadcast_to(
            jnp.sum(per_row, axis=1, keepdims=True), (1, lanes)
        )
    where = jnp.where(good, total + label.astype(jnp.float32) * per_cycle, -1.0)
    for r in range(rows):
        place[r * lanes : (r + 1) * lanes, :] = jnp.broadcast_to(where[r : r + 1], (lanes, lanes)).T


def kernel(
    frame_count, mod_count, frames_hbm, label_hbm, good_hbm, out,
    frames, label, good, place, partial, packed, held, counts, tiles, far,
    in_sem, recv_sem, send_sem, count_send, count_recv, far_send, far_recv,
):
    f = lax.axis_index("frame")
    m = lax.axis_index("mod")
    core = f % 2
    chip = f // 2
    chips = frame_count // 2
    y_count = mod_count // 2
    y, x = m // 2, m % 2
    partner = f + 1 - 2 * core
    steps = 2 * mod_count
    cycles = 2 * mod_count
    rows, per_cycle = packed.shape[1:]

    has_up1, has_up2 = chip + 1 < chips, chip + 2 < chips
    has_dn1, has_dn2 = chip >= 1, chip >= 2

    own, down1, down2, up1, up2 = 4 + core, 6 + core, 8 + core, 2 + core, core
    other_down1, other_down2, other_own = 7 - core, 9 - core, 5 - core

    loads = [
        pltpu.make_async_copy(src, dst, in_sem.at[i])
        for i, (src, dst) in enumerate(
            ((label_hbm, label), (good_hbm, good), (frames_hbm, frames))
        )
    ]
    for load in loads:
        load.start()

    def peer(o, sign):
        dy, dx = o // 2, o % 2
        return ((y + sign * dy + y_count) % y_count) * 2 + (x + dx) % 2

    barrier = pltpu.get_barrier_semaphore()

    def greet(cond, fr, mo):
        @pl.when(cond)
        def _():
            pl.semaphore_signal(barrier, inc=1, device_id=(fr, mo), device_id_type=MESH)

    for o in range(1, mod_count):
        pl.semaphore_signal(barrier, inc=1, device_id=(f, peer(o, 1)), device_id_type=MESH)
    pl.semaphore_signal(barrier, inc=1, device_id=(partner, m), device_id_type=MESH)
    greet(has_up1, f + 2, m)
    greet(has_up2, f + 4, m)
    greet(has_dn1, f - 2, m)
    greet(has_dn2, f - 4, m)
    arrivals = mod_count
    for cond in (has_up1, has_up2, has_dn1, has_dn2):
        arrivals = arrivals + jnp.where(cond, 1, 0)

    loads[0].wait()
    loads[1].wait()
    rank_pixels(label, good, place, partial, cycles, per_cycle)
    loads[2].wait()
    pl.semaphore_wait(barrier, arrivals)

    def remote(src, dst, send, recv, fr, mo):
        return pltpu.make_async_remote_copy(
            src_ref=src, dst_ref=dst, send_sem=send, recv_sem=recv,
            device_id=(fr, mo), device_id_type=MESH,
        )

    def forward(from_slot, to_slot, k, lane, fr):
        remote(
            held.at[from_slot, k], held.at[to_slot, k], send_sem.at[lane],
            recv_sem.at[to_slot, k], fr, m,
        ).start()

    def arrived(slot, k):
        pltpu.make_async_copy(held.at[slot, k], held.at[slot, k], recv_sem.at[slot, k]).wait()

    def arrange(k):
        cyc, o = k // mod_count, k % mod_count
        cycle = 2 * peer(o, -1) + cyc
        lane = lax.broadcasted_iota(jnp.int32, (256, 128), 1) + cycle * per_cycle
        wanted = [(lane + h * 128).astype(jnp.float32) for h in range(per_cycle // 128)]
        total = None
        for r in range(0, frames.shape[1], 256):
            spot = place[r : r + 256, :]
            hot = jnp.concatenate(
                [jnp.where(spot == w, 1.0, 0.0).astype(jnp.bfloat16) for w in wanted], axis=1
            )
            term = jnp.dot(frames[:, r : r + 256], hot, preferred_element_type=jnp.float32)
            total = term if total is None else total + term
        packed[k] = total.astype(jnp.bfloat16)

    def launch(k):
        o = k % mod_count

        @pl.when(o == 0)
        def _():
            pltpu.make_async_copy(packed.at[k], held.at[own, k], recv_sem.at[own, k]).start()

        @pl.when(o > 0)
        def _():
            remote(
                packed.at[k], held.at[own, k], send_sem.at[0], recv_sem.at[own, k], f, peer(o, -1)
            ).start()

    def own_stage(k):
        arrived(own, k)

        @pl.when(has_dn1)
        def _():
            forward(own, down1, k, 1, f - 2)

        @pl.when(has_up1)
        def _():
            forward(own, up1, k, 2, f + 2)

        forward(own, own, k, 3, partner)

    def relay_stage(k):
        @pl.when(has_up1)
        def _():
            arrived(down1, k)

            @pl.when(has_dn1)
            def _():
                forward(down1, down2, k, 4, f - 2)

            forward(down1, down1, k, 5, partner)

        @pl.when(has_dn1)
        def _():
            arrived(up1, k)

            @pl.when(has_up1)
            def _():
                forward(up1, up2, k, 6, f + 2)

    def share_stage(k):
        @pl.when(has_up2)
        def _():
            arrived(down2, k)
            forward(down2, down2, k, 7, partner)

    @pl.loop(0, mod_count + 1)
    def _(o):
        @pl.when(o < mod_count)
        def _():
            arrange(o)

        @pl.when(o >= 1)
        def _():
            launch(o - 1)

        @pl.when(o == 2)
        def _():
            own_stage(0)

    for o in range(mod_count):
        to = peer(o, -1)
        if o == 0:
            pltpu.make_async_copy(partial.at[to], counts.at[o], count_recv.at[o]).start()
        else:
            remote(partial.at[to], counts.at[o], count_send.at[o], count_recv.at[o], f, to).start()

    @pl.loop(1, steps)
    def _(k):
        own_stage(k)

        @pl.when(k <= mod_count)
        def _():
            arrange(mod_count + k - 1)

        @pl.when((k >= 2) & (k <= mod_count + 1))
        def _():
            launch(mod_count + k - 2)

    @pl.loop(0, steps)
    def _(k):
        relay_stage(k)

    def far3_copy(cyc):
        return remote(
            far.at[cyc, pl.ds(0, 2)], tiles.at[cyc, pl.ds(6, 2)],
            far_send.at[cyc, 0], far_recv.at[cyc, 0], f - 2, m,
        )

    def far4_copy(cyc, i):
        return remote(
            far.at[cyc, 2 + i], tiles.at[cyc, 8 + i],
            far_send.at[cyc, 1 + i], far_recv.at[cyc, 1 + i], f - 4, m,
        )

    sends3, sends4 = has_dn1 & has_up2, has_dn2 & has_up2

    def compute(cyc):
        @pl.loop(0, mod_count)
        def _(o):
            k = cyc * mod_count + o
            arrived(other_own, k)

            @pl.when(has_up1)
            def _():
                arrived(other_down1, k)

            @pl.when(has_up2)
            def _():
                arrived(other_down2, k)

            @pl.when(has_dn2)
            def _():
                arrived(up2, k)

        count = counts[0]
        for o in range(1, mod_count):
            count = count + counts[o]
        count = count[cyc : cyc + 1]
        ones = jnp.ones((16, per_cycle), jnp.bfloat16)

        def products(lhs_slots, rhs_slot):
            total = None
            for o in range(mod_count):
                k = cyc * mod_count + o
                lhs = jnp.concatenate([held[s, k] for s in lhs_slots] + [ones], axis=0)
                rhs = held[rhs_slot : rhs_slot + 2, k].reshape(2 * rows, per_cycle)
                term = nt_dot(lhs, rhs)
                total = term if total is None else total + term
            return total

        def row_sums(slot):
            total = None
            for o in range(mod_count):
                block = held[slot, cyc * mod_count + o].astype(jnp.float32)
                total = block if total is None else total + block
            return jnp.sum(total, axis=1, keepdims=True)

        def tile(total, i, earlier, later, half):
            span = slice(half * 128, half * 128 + 128)
            return total[i * 128 : i * 128 + 128, span] * count / (earlier * later[:, span])

        mine = row_sums(own)

        @pl.when(has_up2)
        def _():
            total = products((up1, up2, own), 8)
            later = total[3 * rows : 3 * rows + 1]
            first, second = row_sums(up1), row_sums(up2)
            for half in range(2):
                far[cyc, half] = tile(total, 0, first, later, half)
                far[cyc, 2 + half] = tile(total, 1, second, later, half)
            for half in range(2):
                tiles[cyc, 4 + half] = tile(total, 2, mine, later, half)

        @pl.when(sends4)
        def _():
            far4_copy(cyc, 0).start()

            @pl.when(core == 1)
            def _():
                far4_copy(cyc, 1).start()

        @pl.when(sends3)
        def _():
            far3_copy(cyc).start()

        @pl.when(jnp.logical_not(has_up2))
        def _():
            tiles[cyc, 4:6] = jnp.zeros((2, 128, 128), jnp.float32)

        def near(rhs_slot):
            total = products((own,), rhs_slot)
            for half in range(2):
                tiles[cyc, rhs_slot - 4 + half] = tile(
                    total, 0, mine, total[rows : rows + 1], half
                )

        near(4)

        @pl.when(has_up1)
        def _():
            near(6)

        @pl.when(jnp.logical_not(has_up1))
        def _():
            tiles[cyc, 2:4] = jnp.zeros((2, 128, 128), jnp.float32)

    def finish(cyc):
        @pl.when(chip + 3 < chips)
        def _():
            far3_copy(cyc).wait_recv()

        @pl.when(chip + 3 >= chips)
        def _():
            tiles[cyc, 6:8] = jnp.zeros((2, 128, 128), jnp.float32)

        @pl.when(chip + 4 < chips)
        def _():
            far4_copy(cyc, 0).wait_recv()

            @pl.when(core == 1)
            def _():
                far4_copy(cyc, 1).wait_recv()

        @pl.when(chip + 4 >= chips)
        def _():
            tiles[cyc, 8:10] = jnp.zeros((2, 128, 128), jnp.float32)

        row = lax.broadcasted_iota(jnp.int32, (128, 128), 0)
        lane = lax.broadcasted_iota(jnp.int32, (128, 128), 1)
        inside = lane + row < 128

        def turned(j):
            piece = tiles[cyc, core + j]
            for bit in (1, 2, 4):
                piece = jnp.where(row // bit % 2 == 1, pltpu.roll(piece, 128 - bit, 1), piece)
            return jnp.concatenate(
                [piece[:8]] + [pltpu.roll(piece[r : r + 8], 128 - r, 1) for r in range(8, 128, 8)],
                axis=0,
            )

        now = turned(0)
        for j in range(LAG // 128):
            later = turned(j + 1)
            out[cyc, :, j * 128 : j * 128 + 128] = jnp.where(inside, now, later)
            now = later

    @pl.loop(0, mod_count)
    def _(k):
        share_stage(k)

    for o in range(mod_count):
        pltpu.make_async_copy(counts.at[o], counts.at[o], count_recv.at[o]).wait()
    compute(0)

    @pl.loop(mod_count, steps)
    def _(k):
        share_stage(k)

    finish(0)
    compute(1)
    finish(1)

    def sent(lane, slot):
        pltpu.make_async_copy(held.at[slot], held.at[slot], send_sem.at[lane]).wait()

    for cyc in range(2):
        part = held.at[own, pl.ds(cyc * mod_count + 1, mod_count - 1)]
        pltpu.make_async_copy(part, part, send_sem.at[0]).wait()
    for o in range(1, mod_count):
        pltpu.make_async_copy(counts.at[o], counts.at[o], count_send.at[o]).wait()
    for lane, slot, cond in (
        (1, own, has_dn1), (2, own, has_up1), (3, own, None), (4, down1, has_up1 & has_dn1),
        (5, down1, has_up1), (6, up1, has_up1 & has_dn1), (7, down2, has_up2),
    ):
        if cond is None:
            sent(lane, slot)
        else:
            pl.when(cond)(functools.partial(sent, lane, slot))
    for cyc in range(2):
        @pl.when(sends3)
        def _():
            far3_copy(cyc).wait_send()

        @pl.when(sends4)
        def _():
            far4_copy(cyc, 0).wait_send()

            @pl.when(core == 1)
            def _():
                far4_copy(cyc, 1).wait_send()


def shards(frames, cycle_label, good_pixel):
    frame_count, mod_count = lax.axis_size("frame"), lax.axis_size("mod")
    rows, pixels = frames.shape
    steps = 2 * mod_count
    per_cycle = pixels // steps
    small = (pixels // 128, 128)
    return pl.pallas_call(
        functools.partial(kernel, frame_count, mod_count),
        out_shape=jax.ShapeDtypeStruct((2, rows, LAG), jnp.float32),
        in_specs=[pl.BlockSpec(memory_space=pl.ANY)] * 3,
        out_specs=pl.BlockSpec(memory_space=pltpu.VMEM),
        scratch_shapes=[
            pltpu.VMEM((rows, pixels), jnp.bfloat16),
            pltpu.VMEM(small, jnp.int32),
            pltpu.VMEM(small, jnp.int32),
            pltpu.VMEM((pixels, 128), jnp.float32),
            pltpu.VMEM((mod_count, 8, 128), jnp.float32),
            pltpu.VMEM((steps, rows, per_cycle), jnp.bfloat16),
            pltpu.VMEM((10, steps, rows, per_cycle), jnp.bfloat16),
            pltpu.VMEM((mod_count, 8, 128), jnp.float32),
            pltpu.VMEM((2, 10, 128, 128), jnp.float32),
            pltpu.VMEM((2, 4, 128, 128), jnp.float32),
            pltpu.SemaphoreType.DMA((3,)),
            pltpu.SemaphoreType.DMA((10, steps)),
            pltpu.SemaphoreType.DMA((8,)),
            pltpu.SemaphoreType.DMA((mod_count,)),
            pltpu.SemaphoreType.DMA((mod_count,)),
            pltpu.SemaphoreType.DMA((2, 3)),
            pltpu.SemaphoreType.DMA((2, 3)),
        ],
        compiler_params=pltpu.CompilerParams(
            collective_id=0, has_side_effects=True, vmem_limit_bytes=32 * 1024 * 1024
        ),
    )(frames, cycle_label.reshape(small), good_pixel.reshape(small))


def solution(mesh):
    placed = (P("frame", "mod"), P("mod"), P("mod"))
    return jax.shard_map(
        shards, mesh=mesh, in_specs=placed, out_specs=P("mod", "frame", None), check_vma=False
    )
```

```python
import functools

import jax
import jax.numpy as jnp
from jax import lax
from jax.experimental import pallas as pl
from jax.experimental.pallas import tpu as pltpu
from jax.sharding import PartitionSpec as P

CYCLES = 16
LAG = 1024
MESH = pl.DeviceIdType.MESH
TRANSIT_LAG = 2
NT = (((1,), (1,)), ((), ()))


def nt_dot(a, b):
    return lax.dot_general(a, b, NT, preferred_element_type=jnp.float32)


def rank_pixels(label_ref, good_ref, place, partial, cycles, per_cycle):
    rows, lanes = label_ref.shape
    label = label_ref[...]
    good = good_ref[...] > 0
    member = jnp.concatenate([jnp.where(label == c, 1.0, 0.0) for c in range(cycles)], axis=0)
    before = lax.broadcasted_iota(jnp.int32, (lanes, lanes), 0)
    at = lax.broadcasted_iota(jnp.int32, (lanes, lanes), 1)
    upper = jnp.where(before < at, 1.0, 0.0).astype(jnp.bfloat16)
    ones = jnp.ones((lanes, lanes), jnp.bfloat16)
    packed = member.astype(jnp.bfloat16)
    in_row = jnp.dot(packed, upper, preferred_element_type=jnp.float32)
    totals = jnp.dot(packed, ones, preferred_element_type=jnp.float32).astype(jnp.bfloat16)
    size = cycles * rows
    here = lax.broadcasted_iota(jnp.int32, (size, size), 0)
    there = lax.broadcasted_iota(jnp.int32, (size, size), 1)
    earlier = jnp.where((here // rows == there // rows) & (there < here), 1.0, 0.0)
    above = jnp.dot(earlier.astype(jnp.bfloat16), totals, preferred_element_type=jnp.float32)
    ranks = (in_row + above) * member
    usable = jnp.where(good, 1.0, 0.0)
    partial[...] = jnp.zeros_like(partial)
    total = None
    for c in range(cycles):
        mine = slice(c * rows, (c + 1) * rows)
        total = ranks[mine] if total is None else total + ranks[mine]
        per_row = jnp.sum(member[mine] * usable, axis=0, keepdims=True)
        partial[c // 2, c % 2 : c % 2 + 1, :] = jnp.broadcast_to(
            jnp.sum(per_row, axis=1, keepdims=True), (1, lanes)
        )
    where = jnp.where(good, total + label.astype(jnp.float32) * per_cycle, -1.0)
    for r in range(rows):
        place[r * lanes : (r + 1) * lanes, :] = jnp.broadcast_to(where[r : r + 1], (lanes, lanes)).T


def kernel(
    frame_count, mod_count, frames_hbm, label_hbm, good_hbm, out,
    frames, label, good, place, partial, packed, held, counts, tiles, far,
    in_sem, recv_sem, send_sem, count_send, count_recv, far_send, far_recv,
):
    f = lax.axis_index("frame")
    m = lax.axis_index("mod")
    core = f % 2
    chip = f // 2
    chips = frame_count // 2
    y_count = mod_count // 2
    y, x = m // 2, m % 2
    partner = f + 1 - 2 * core
    steps = 2 * mod_count
    cycles = 2 * mod_count
    rows, per_cycle = packed.shape[1:]

    has_up1, has_up2 = chip + 1 < chips, chip + 2 < chips
    has_dn1, has_dn2 = chip >= 1, chip >= 2

    own, down1, down2, up1, up2 = 4 + core, 6 + core, 8 + core, 2 + core, core
    other_down1, other_down2, other_own = 7 - core, 9 - core, 5 - core

    loads = [
        pltpu.make_async_copy(src, dst, in_sem.at[i])
        for i, (src, dst) in enumerate(
            ((label_hbm, label), (good_hbm, good), (frames_hbm, frames))
        )
    ]
    for load in loads:
        load.start()

    half = chips // 2
    first, last = chip == 0, chip == chips - 1
    below, above = chip == half - 1, chip == half
    at_first, at_last = core, frame_count - 2 + core
    at_below, at_above = 2 * half - 2 + core, 2 * half + core

    def peer(o, sign):
        dy, dx = o // 2, o % 2
        return ((y + sign * dy + y_count) % y_count) * 2 + (x + dx) % 2

    barrier = pltpu.get_barrier_semaphore()

    def greet(cond, fr, mo):
        @pl.when(cond)
        def _():
            pl.semaphore_signal(barrier, inc=1, device_id=(fr, mo), device_id_type=MESH)

    for o in range(1, mod_count):
        pl.semaphore_signal(barrier, inc=1, device_id=(f, peer(o, 1)), device_id_type=MESH)
    pl.semaphore_signal(barrier, inc=1, device_id=(partner, m), device_id_type=MESH)
    greet(has_up1, f + 2, m)
    greet(has_up2, f + 4, m)
    greet(has_dn1, f - 2, m)
    greet(has_dn2, f - 4, m)
    for ends, targets in (
        (first | last, (at_below, at_above)), (below | above, (at_first, at_last))
    ):
        for target in targets:
            greet(ends, target, m)
    arrivals = mod_count
    ends = first | last | below | above
    for cond in (has_up1, has_up2, has_dn1, has_dn2, ends, ends):
        arrivals = arrivals + jnp.where(cond, 1, 0)

    loads[0].wait()
    loads[1].wait()
    rank_pixels(label, good, place, partial, cycles, per_cycle)
    loads[2].wait()
    pl.semaphore_wait(barrier, arrivals)

    def remote(src, dst, send, recv, fr, mo):
        return pltpu.make_async_remote_copy(
            src_ref=src, dst_ref=dst, send_sem=send, recv_sem=recv,
            device_id=(fr, mo), device_id_type=MESH,
        )

    def forward(from_slot, to_slot, k, lane, fr):
        remote(
            held.at[from_slot, k], held.at[to_slot, k], send_sem.at[lane],
            recv_sem.at[to_slot, k], fr, m,
        ).start()

    def arrived(slot, k):
        pltpu.make_async_copy(held.at[slot, k], held.at[slot, k], recv_sem.at[slot, k]).wait()

    def arrange(k):
        cyc, o = k // mod_count, k % mod_count
        cycle = 2 * peer(o, -1) + cyc
        lane = lax.broadcasted_iota(jnp.int32, (256, 128), 1) + cycle * per_cycle
        wanted = [(lane + h * 128).astype(jnp.float32) for h in range(per_cycle // 128)]
        total = None
        for r in range(0, frames.shape[1], 256):
            spot = place[r : r + 256, :]
            hot = jnp.concatenate(
                [jnp.where(spot == w, 1.0, 0.0).astype(jnp.bfloat16) for w in wanted], axis=1
            )
            term = jnp.dot(frames[:, r : r + 256], hot, preferred_element_type=jnp.float32)
            total = term if total is None else total + term
        packed[k] = total.astype(jnp.bfloat16)

    def launch(k):
        o = k % mod_count

        @pl.when(o == 0)
        def _():
            pltpu.make_async_copy(packed.at[k], held.at[own, k], recv_sem.at[own, k]).start()

        @pl.when(o > 0)
        def _():
            remote(
                packed.at[k], held.at[own, k], send_sem.at[0], recv_sem.at[own, k], f, peer(o, -1)
            ).start()

    def forward_down(from_slot, to_slot, by_slot, k, lane):
        detour = above & (k % 2 == 1)

        @pl.when(detour)
        def _():
            forward(from_slot, by_slot, k, lane, at_first)

        @pl.when(has_dn1 & jnp.logical_not(detour))
        def _():
            forward(from_slot, to_slot, k, lane, f - 2)

    def forward_up(from_slot, to_slot, by_slot, k, lane):
        detour = below & (k % 2 == 1)

        @pl.when(detour)
        def _():
            forward(from_slot, by_slot, k, lane, at_last)

        @pl.when(has_up1 & jnp.logical_not(detour))
        def _():
            forward(from_slot, to_slot, k, lane, f + 2)

    def transit(up_slot, down_slot, k, lane):
        @pl.when(first)
        def _():
            arrived(up_slot, k)
            forward(up_slot, down_slot, k, lane, at_below)

        @pl.when(last)
        def _():
            arrived(down_slot, k)
            forward(down_slot, up_slot, k, lane, at_above)

    def own_stage(k):
        arrived(own, k)
        forward_down(own, down1, up1, k, 1)
        forward_up(own, up1, down1, k, 2)
        forward(own, own, k, 3, partner)

    def relay_stage(k):
        @pl.when(has_up1)
        def _():
            arrived(down1, k)
            forward_down(down1, down2, up2, k, 4)
            forward(down1, down1, k, 5, partner)

        @pl.when(has_dn1)
        def _():
            arrived(up1, k)
            forward_up(up1, up2, down2, k, 6)

    def share_stage(k):
        @pl.when(has_up2)
        def _():
            arrived(down2, k)
            forward(down2, down2, k, 7, partner)

    @pl.loop(0, mod_count + 1)
    def _(o):
        @pl.when(o < mod_count)
        def _():
            arrange(o)

        @pl.when(o >= 1)
        def _():
            launch(o - 1)

        @pl.when(o == 2)
        def _():
            own_stage(0)

    for o in range(mod_count):
        to = peer(o, -1)
        if o == 0:
            pltpu.make_async_copy(partial.at[to], counts.at[o], count_recv.at[o]).start()
        else:
            remote(partial.at[to], counts.at[o], count_send.at[o], count_recv.at[o], f, to).start()

    @pl.loop(1, steps)
    def _(k):
        own_stage(k)

        @pl.when(k <= mod_count)
        def _():
            arrange(mod_count + k - 1)

        @pl.when((k >= 2) & (k <= mod_count + 1))
        def _():
            launch(mod_count + k - 2)

        @pl.when((k > TRANSIT_LAG) & (k % 2 == 1))
        def _():
            transit(up1, down1, k - TRANSIT_LAG, 8)

    @pl.loop(0, steps)
    def _(k):
        relay_stage(k)

        @pl.when((k < TRANSIT_LAG) & (k % 2 == 1))
        def _():
            transit(up1, down1, steps - TRANSIT_LAG + k, 8)

        @pl.when((k > TRANSIT_LAG) & (k % 2 == 1))
        def _():
            transit(up2, down2, k - TRANSIT_LAG, 9)

    def far3_copy(cyc):
        return remote(
            far.at[cyc, pl.ds(0, 2)], tiles.at[cyc, pl.ds(6, 2)],
            far_send.at[cyc, 0], far_recv.at[cyc, 0], f - 2, m,
        )

    def far4_copy(cyc, i):
        return remote(
            far.at[cyc, 2 + i], tiles.at[cyc, 8 + i],
            far_send.at[cyc, 1 + i], far_recv.at[cyc, 1 + i], f - 4, m,
        )

    sends3, sends4 = has_dn1 & has_up2, has_dn2 & has_up2

    def compute(cyc):
        @pl.loop(0, mod_count)
        def _(o):
            k = cyc * mod_count + o
            arrived(other_own, k)

            @pl.when(has_up1)
            def _():
                arrived(other_down1, k)

            @pl.when(has_up2)
            def _():
                arrived(other_down2, k)

            @pl.when(has_dn2)
            def _():
                arrived(up2, k)

        count = counts[0]
        for o in range(1, mod_count):
            count = count + counts[o]
        count = count[cyc : cyc + 1]
        ones = jnp.ones((16, per_cycle), jnp.bfloat16)

        def products(lhs_slots, rhs_slot):
            total = None
            for o in range(mod_count):
                k = cyc * mod_count + o
                lhs = jnp.concatenate([held[s, k] for s in lhs_slots] + [ones], axis=0)
                rhs = held[rhs_slot : rhs_slot + 2, k].reshape(2 * rows, per_cycle)
                term = nt_dot(lhs, rhs)
                total = term if total is None else total + term
            return total

        def row_sums(slot):
            total = None
            for o in range(mod_count):
                block = held[slot, cyc * mod_count + o].astype(jnp.float32)
                total = block if total is None else total + block
            return jnp.sum(total, axis=1, keepdims=True)

        def tile(total, i, earlier, later, half):
            span = slice(half * 128, half * 128 + 128)
            return total[i * 128 : i * 128 + 128, span] * count / (earlier * later[:, span])

        mine = row_sums(own)

        @pl.when(has_up2)
        def _():
            total = products((up1, up2, own), 8)
            later = total[3 * rows : 3 * rows + 1]
            first, second = row_sums(up1), row_sums(up2)
            for half in range(2):
                far[cyc, half] = tile(total, 0, first, later, half)
                far[cyc, 2 + half] = tile(total, 1, second, later, half)
            for half in range(2):
                tiles[cyc, 4 + half] = tile(total, 2, mine, later, half)

        @pl.when(sends4)
        def _():
            far4_copy(cyc, 0).start()

            @pl.when(core == 1)
            def _():
                far4_copy(cyc, 1).start()

        @pl.when(sends3)
        def _():
            far3_copy(cyc).start()

        @pl.when(jnp.logical_not(has_up2))
        def _():
            tiles[cyc, 4:6] = jnp.zeros((2, 128, 128), jnp.float32)

        def near(rhs_slot):
            total = products((own,), rhs_slot)
            for half in range(2):
                tiles[cyc, rhs_slot - 4 + half] = tile(
                    total, 0, mine, total[rows : rows + 1], half
                )

        near(4)

        @pl.when(has_up1)
        def _():
            near(6)

        @pl.when(jnp.logical_not(has_up1))
        def _():
            tiles[cyc, 2:4] = jnp.zeros((2, 128, 128), jnp.float32)

    def finish(cyc):
        @pl.when(chip + 3 < chips)
        def _():
            far3_copy(cyc).wait_recv()

        @pl.when(chip + 3 >= chips)
        def _():
            tiles[cyc, 6:8] = jnp.zeros((2, 128, 128), jnp.float32)

        @pl.when(chip + 4 < chips)
        def _():
            far4_copy(cyc, 0).wait_recv()

            @pl.when(core == 1)
            def _():
                far4_copy(cyc, 1).wait_recv()

        @pl.when(chip + 4 >= chips)
        def _():
            tiles[cyc, 8:10] = jnp.zeros((2, 128, 128), jnp.float32)

        row = lax.broadcasted_iota(jnp.int32, (128, 128), 0)
        lane = lax.broadcasted_iota(jnp.int32, (128, 128), 1)
        inside = lane + row < 128

        def turned(j):
            piece = tiles[cyc, core + j]
            for bit in (1, 2, 4):
                piece = jnp.where(row // bit % 2 == 1, pltpu.roll(piece, 128 - bit, 1), piece)
            return jnp.concatenate(
                [piece[:8]] + [pltpu.roll(piece[r : r + 8], 128 - r, 1) for r in range(8, 128, 8)],
                axis=0,
            )

        now = turned(0)
        for j in range(LAG // 128):
            later = turned(j + 1)
            out[cyc, :, j * 128 : j * 128 + 128] = jnp.where(inside, now, later)
            now = later

    @pl.loop(0, mod_count)
    def _(k):
        @pl.when((k < TRANSIT_LAG) & (k % 2 == 1))
        def _():
            transit(up2, down2, steps - TRANSIT_LAG + k, 9)

        share_stage(k)

    for o in range(mod_count):
        pltpu.make_async_copy(counts.at[o], counts.at[o], count_recv.at[o]).wait()
    compute(0)

    @pl.loop(mod_count, steps)
    def _(k):
        share_stage(k)

    finish(0)
    compute(1)
    finish(1)

    def sent(lane, slot):
        pltpu.make_async_copy(held.at[slot], held.at[slot], send_sem.at[lane]).wait()

    def sent_half(lane, slot):
        part = held.at[slot, pl.ds(0, mod_count)]
        pltpu.make_async_copy(part, part, send_sem.at[lane]).wait()

    @pl.when(first | last)
    def _():
        sent_half(8, up1)
        sent_half(9, up2)

    for cyc in range(2):
        part = held.at[own, pl.ds(cyc * mod_count + 1, mod_count - 1)]
        pltpu.make_async_copy(part, part, send_sem.at[0]).wait()
    for o in range(1, mod_count):
        pltpu.make_async_copy(counts.at[o], counts.at[o], count_send.at[o]).wait()
    for lane, slot, cond in (
        (1, own, has_dn1), (2, own, has_up1), (3, own, None), (4, down1, has_up1 & has_dn1),
        (5, down1, has_up1), (6, up1, has_up1 & has_dn1), (7, down2, has_up2),
    ):
        if cond is None:
            sent(lane, slot)
        else:
            pl.when(cond)(functools.partial(sent, lane, slot))
    for cyc in range(2):
        @pl.when(sends3)
        def _():
            far3_copy(cyc).wait_send()

        @pl.when(sends4)
        def _():
            far4_copy(cyc, 0).wait_send()

            @pl.when(core == 1)
            def _():
                far4_copy(cyc, 1).wait_send()


def shards(frames, cycle_label, good_pixel):
    frame_count, mod_count = lax.axis_size("frame"), lax.axis_size("mod")
    rows, pixels = frames.shape
    steps = 2 * mod_count
    per_cycle = pixels // steps
    small = (pixels // 128, 128)
    return pl.pallas_call(
        functools.partial(kernel, frame_count, mod_count),
        out_shape=jax.ShapeDtypeStruct((2, rows, LAG), jnp.float32),
        in_specs=[pl.BlockSpec(memory_space=pl.ANY)] * 3,
        out_specs=pl.BlockSpec(memory_space=pltpu.VMEM),
        scratch_shapes=[
            pltpu.VMEM((rows, pixels), jnp.bfloat16),
            pltpu.VMEM(small, jnp.int32),
            pltpu.VMEM(small, jnp.int32),
            pltpu.VMEM((pixels, 128), jnp.float32),
            pltpu.VMEM((mod_count, 8, 128), jnp.float32),
            pltpu.VMEM((steps, rows, per_cycle), jnp.bfloat16),
            pltpu.VMEM((10, steps, rows, per_cycle), jnp.bfloat16),
            pltpu.VMEM((mod_count, 8, 128), jnp.float32),
            pltpu.VMEM((2, 10, 128, 128), jnp.float32),
            pltpu.VMEM((2, 4, 128, 128), jnp.float32),
            pltpu.SemaphoreType.DMA((3,)),
            pltpu.SemaphoreType.DMA((10, steps)),
            pltpu.SemaphoreType.DMA((10,)),
            pltpu.SemaphoreType.DMA((mod_count,)),
            pltpu.SemaphoreType.DMA((mod_count,)),
            pltpu.SemaphoreType.DMA((2, 3)),
            pltpu.SemaphoreType.DMA((2, 3)),
        ],
        compiler_params=pltpu.CompilerParams(
            collective_id=0, has_side_effects=True, vmem_limit_bytes=32 * 1024 * 1024
        ),
    )(frames, cycle_label.reshape(small), good_pixel.reshape(small))


def solution(mesh):
    placed = (P("frame", "mod"), P("mod"), P("mod"))
    return jax.shard_map(
        shards, mesh=mesh, in_specs=placed, out_specs=P("mod", "frame", None), check_vma=False
    )
```

```python
import functools

import jax
import jax.numpy as jnp
from jax import lax
from jax.experimental import pallas as pl
from jax.experimental.pallas import tpu as pltpu
from jax.sharding import PartitionSpec as P

CYCLES = 16
LAG = 1024
MESH = pl.DeviceIdType.MESH
TRANSIT_LAG = 2
OWN_LAG = 6
CODE = 5600.0
NT = (((1,), (1,)), ((), ()))


def nt_dot(a, b):
    return lax.dot_general(a, b, NT, preferred_element_type=jnp.float32)


def rank_pixels(label_ref, good_ref, place, partial, cycles, per_cycle):
    rows, lanes = label_ref.shape
    label = label_ref[...]
    good = good_ref[...] > 0
    member = jnp.concatenate([jnp.where(label == c, 1.0, 0.0) for c in range(cycles)], axis=0)
    before = lax.broadcasted_iota(jnp.int32, (lanes, lanes), 0)
    at = lax.broadcasted_iota(jnp.int32, (lanes, lanes), 1)
    upper = jnp.where(before < at, 1.0, 0.0).astype(jnp.bfloat16)
    ones = jnp.ones((lanes, lanes), jnp.bfloat16)
    packed = member.astype(jnp.bfloat16)
    in_row = jnp.dot(packed, upper, preferred_element_type=jnp.float32)
    totals = jnp.dot(packed, ones, preferred_element_type=jnp.float32).astype(jnp.bfloat16)
    size = cycles * rows
    here = lax.broadcasted_iota(jnp.int32, (size, size), 0)
    there = lax.broadcasted_iota(jnp.int32, (size, size), 1)
    earlier = jnp.where((here // rows == there // rows) & (there < here), 1.0, 0.0)
    above = jnp.dot(earlier.astype(jnp.bfloat16), totals, preferred_element_type=jnp.float32)
    ranks = (in_row + above) * member
    usable = jnp.where(good, 1.0, 0.0)
    partial[...] = jnp.zeros_like(partial)
    total = None
    for c in range(cycles):
        mine = slice(c * rows, (c + 1) * rows)
        total = ranks[mine] if total is None else total + ranks[mine]
        per_row = jnp.sum(member[mine] * usable, axis=0, keepdims=True)
        partial[c // 2, c % 2 : c % 2 + 1, :] = jnp.broadcast_to(
            jnp.sum(per_row, axis=1, keepdims=True), (1, lanes)
        )
    where = jnp.where(good, total + label.astype(jnp.float32) * per_cycle, -1.0)
    for r in range(rows):
        place[r * lanes : (r + 1) * lanes, :] = jnp.broadcast_to(where[r : r + 1], (lanes, lanes)).T


def kernel(
    frame_count, mod_count, frames_hbm, label_hbm, good_hbm, out,
    frames, label, good, place, partial, packed, held, counts, tiles, far, code,
    in_sem, recv_sem, send_sem, count_send, count_recv, far_send, far_recv,
):
    f = lax.axis_index("frame")
    m = lax.axis_index("mod")
    core = f % 2
    chip = f // 2
    chips = frame_count // 2
    y_count = mod_count // 2
    y, x = m // 2, m % 2
    partner = f + 1 - 2 * core
    steps = 2 * mod_count
    cycles = 2 * mod_count
    rows, per_cycle = packed.shape[1:]

    has_up1, has_up2 = chip + 1 < chips, chip + 2 < chips
    has_dn1, has_dn2 = chip >= 1, chip >= 2

    own, down1, down2, up1, up2 = 4 + core, 6 + core, 8 + core, 2 + core, core
    other_down1, other_down2, other_own = 7 - core, 9 - core, 5 - core

    loads = [
        pltpu.make_async_copy(src, dst, in_sem.at[i])
        for i, (src, dst) in enumerate(
            ((label_hbm, label), (good_hbm, good), (frames_hbm, frames))
        )
    ]
    for load in loads:
        load.start()

    half = chips // 2
    first, last = chip == 0, chip == chips - 1
    below, above = chip == half - 1, chip == half
    at_first, at_last = core, frame_count - 2 + core
    at_below, at_above = 2 * half - 2 + core, 2 * half + core

    def peer(o, sign):
        dy, dx = o // 2, o % 2
        return ((y + sign * dy + y_count) % y_count) * 2 + (x + dx) % 2

    barrier = pltpu.get_barrier_semaphore()

    def greet(cond, fr, mo):
        @pl.when(cond)
        def _():
            pl.semaphore_signal(barrier, inc=1, device_id=(fr, mo), device_id_type=MESH)

    for o in range(1, mod_count):
        pl.semaphore_signal(barrier, inc=1, device_id=(f, peer(o, 1)), device_id_type=MESH)
    pl.semaphore_signal(barrier, inc=1, device_id=(partner, m), device_id_type=MESH)
    greet(has_up1, f + 2, m)
    greet(has_up2, f + 4, m)
    greet(has_dn1, f - 2, m)
    greet(has_dn2, f - 4, m)
    for ends, targets in (
        (first | last, (at_below, at_above)), (below | above, (at_first, at_last))
    ):
        for target in targets:
            greet(ends, target, m)
    arrivals = mod_count
    ends = first | last | below | above
    for cond in (has_up1, has_up2, has_dn1, has_dn2, ends, ends):
        arrivals = arrivals + jnp.where(cond, 1, 0)

    loads[0].wait()
    loads[1].wait()
    rank_pixels(label, good, place, partial, cycles, per_cycle)
    loads[2].wait()
    pl.semaphore_wait(barrier, arrivals)

    def remote(src, dst, send, recv, fr, mo):
        return pltpu.make_async_remote_copy(
            src_ref=src, dst_ref=dst, send_sem=send, recv_sem=recv,
            device_id=(fr, mo), device_id_type=MESH,
        )

    def forward(from_slot, to_slot, k, lane, fr):
        remote(
            held.at[from_slot, k], held.at[to_slot, k], send_sem.at[lane],
            recv_sem.at[to_slot, k], fr, m,
        ).start()

    def arrived(slot, k):
        pltpu.make_async_copy(held.at[slot, k], held.at[slot, k], recv_sem.at[slot, k]).wait()

    def arrange(k):
        cyc, o = k // mod_count, k % mod_count
        cycle = 2 * peer(o, -1) + cyc
        lane = lax.broadcasted_iota(jnp.int32, (256, 128), 1) + cycle * per_cycle
        wanted = [(lane + h * 128).astype(jnp.float32) for h in range(per_cycle // 128)]
        total = None
        for r in range(0, frames.shape[1], 256):
            spot = place[r : r + 256, :]
            hot = jnp.concatenate(
                [jnp.where(spot == w, 1.0, 0.0).astype(jnp.bfloat16) for w in wanted], axis=1
            )
            term = jnp.dot(frames[:, r : r + 256], hot, preferred_element_type=jnp.float32)
            total = term if total is None else total + term
        packed[k] = total.astype(jnp.bfloat16)

    def launch(k):
        o = k % mod_count

        @pl.when(o == 0)
        def _():
            pltpu.make_async_copy(packed.at[k], held.at[own, k], recv_sem.at[own, k]).start()

        @pl.when(o > 0)
        def _():
            remote(
                packed.at[k], held.at[own, k], send_sem.at[0], recv_sem.at[own, k], f, peer(o, -1)
            ).start()

    def forward_down(from_slot, to_slot, by_slot, k, lane):
        detour = above & (k % 2 == 1)

        @pl.when(detour)
        def _():
            forward(from_slot, by_slot, k, lane, at_first)

        @pl.when(has_dn1 & jnp.logical_not(detour))
        def _():
            forward(from_slot, to_slot, k, lane, f - 2)

    def forward_up(from_slot, to_slot, by_slot, k, lane):
        detour = below & (k % 2 == 1)

        @pl.when(detour)
        def _():
            forward(from_slot, by_slot, k, lane, at_last)

        @pl.when(has_up1 & jnp.logical_not(detour))
        def _():
            forward(from_slot, to_slot, k, lane, f + 2)

    def transit(up_slot, down_slot, k, lane):
        @pl.when(first)
        def _():
            arrived(up_slot, k)
            forward(up_slot, down_slot, k, lane, at_below)

        @pl.when(last)
        def _():
            arrived(down_slot, k)
            forward(down_slot, up_slot, k, lane, at_above)

    def own_stage(k):
        arrived(own, k)
        forward_down(own, down1, up1, k, 1)
        forward_up(own, up1, down1, k, 2)
        forward(own, own, k, 3, partner)

    def relay_stage(k):
        @pl.when(has_up1)
        def _():
            arrived(down1, k)
            forward_down(down1, down2, up2, k, 4)
            forward(down1, down1, k, 5, partner)

        @pl.when(has_dn1)
        def _():
            arrived(up1, k)
            forward_up(up1, up2, down2, k, 6)

    def share_stage(k):
        @pl.when(has_up2)
        def _():
            arrived(down2, k)
            forward(down2, down2, k, 7, partner)

    for o in range(mod_count):
        to = peer(o, -1)
        if o == 0:
            pltpu.make_async_copy(partial.at[to], counts.at[o], count_recv.at[o]).start()
        else:
            remote(partial.at[to], counts.at[o], count_send.at[o], count_recv.at[o], f, to).start()

    def slab(i):
        early = jnp.where(i == 1, mod_count, i - 1)
        return jnp.where((i >= 1) & (i <= mod_count), early, i)

    @pl.loop(0, steps + OWN_LAG + TRANSIT_LAG)
    def _(i):
        @pl.when(i < steps)
        def _():
            arrange(slab(i))

        @pl.when((i >= 1) & (i <= steps))
        def _():
            launch(slab(i - 1))

        @pl.when((i >= 2) & (i < 4))
        def _():
            own_stage(slab(i - 2))

        @pl.when((i >= OWN_LAG + 2) & (i < steps + OWN_LAG))
        def _():
            own_stage(slab(i - OWN_LAG))

        passed = slab(i - OWN_LAG - TRANSIT_LAG)

        @pl.when((i >= OWN_LAG + TRANSIT_LAG) & (passed % 2 == 1))
        def _():
            transit(up1, down1, passed, 8)

    @pl.loop(0, steps)
    def _(k):
        relay_stage(k)

        @pl.when((k > TRANSIT_LAG) & (k % 2 == 1))
        def _():
            transit(up2, down2, k - TRANSIT_LAG, 9)

    def far3_copy(cyc):
        return remote(
            far.at[cyc, pl.ds(0, 2)], code.at[cyc, pl.ds(0, 2)],
            far_send.at[cyc, 0], far_recv.at[cyc, 0], f - 2, m,
        )

    def far4_copy(cyc, i):
        return remote(
            far.at[cyc, 2 + i], code.at[cyc, 2 + i],
            far_send.at[cyc, 1 + i], far_recv.at[cyc, 1 + i], f - 4, m,
        )

    sends3, sends4 = has_dn1 & has_up2, has_dn2 & has_up2

    def compute(cyc):
        @pl.loop(0, mod_count)
        def _(o):
            k = cyc * mod_count + o
            arrived(other_own, k)

            @pl.when(has_up1)
            def _():
                arrived(other_down1, k)

            @pl.when(has_up2)
            def _():
                arrived(other_down2, k)

            @pl.when(has_dn2)
            def _():
                arrived(up2, k)

        count = counts[0]
        for o in range(1, mod_count):
            count = count + counts[o]
        count = count[cyc : cyc + 1]
        ones = jnp.ones((16, per_cycle), jnp.bfloat16)

        def products(lhs_slots, rhs_slot):
            total = None
            for o in range(mod_count):
                k = cyc * mod_count + o
                lhs = jnp.concatenate([held[s, k] for s in lhs_slots] + [ones], axis=0)
                rhs = held[rhs_slot : rhs_slot + 2, k].reshape(2 * rows, per_cycle)
                term = nt_dot(lhs, rhs)
                total = term if total is None else total + term
            return total

        def row_sums(slot):
            total = None
            for o in range(mod_count):
                block = held[slot, cyc * mod_count + o].astype(jnp.float32)
                total = block if total is None else total + block
            return jnp.sum(total, axis=1, keepdims=True)

        def coded(value):
            return jnp.round(jnp.log(value) * CODE).astype(jnp.int32).astype(jnp.int16)

        def tile(total, i, earlier, later, half):
            span = slice(half * 128, half * 128 + 128)
            return total[i * 128 : i * 128 + 128, span] * count / (earlier * later[:, span])

        mine = row_sums(own)

        @pl.when(has_up2)
        def _():
            total = products((up1, up2, own), 8)
            later = total[3 * rows : 3 * rows + 1]
            first, second = row_sums(up1), row_sums(up2)
            for half in range(2):
                far[cyc, half] = coded(tile(total, 0, first, later, half))
                far[cyc, 2 + half] = coded(tile(total, 1, second, later, half))
            for half in range(2):
                tiles[cyc, 4 + half] = tile(total, 2, mine, later, half)

        @pl.when(sends4)
        def _():
            far4_copy(cyc, 0).start()

            @pl.when(core == 1)
            def _():
                far4_copy(cyc, 1).start()

        @pl.when(sends3)
        def _():
            far3_copy(cyc).start()

        @pl.when(jnp.logical_not(has_up2))
        def _():
            tiles[cyc, 4:6] = jnp.zeros((2, 128, 128), jnp.float32)

        def near(rhs_slot):
            total = products((own,), rhs_slot)
            for half in range(2):
                tiles[cyc, rhs_slot - 4 + half] = tile(
                    total, 0, mine, total[rows : rows + 1], half
                )

        near(4)

        @pl.when(has_up1)
        def _():
            near(6)

        @pl.when(jnp.logical_not(has_up1))
        def _():
            tiles[cyc, 2:4] = jnp.zeros((2, 128, 128), jnp.float32)

    def finish(cyc):
        def decode(i):
            value = code[cyc, i].astype(jnp.int32).astype(jnp.float32)
            tiles[cyc, 6 + i] = jnp.exp(value * (1.0 / CODE))

        def clear(i):
            tiles[cyc, 6 + i] = jnp.zeros((128, 128), jnp.float32)

        @pl.when(chip + 3 < chips)
        def _():
            far3_copy(cyc).wait_recv()
            decode(0)
            decode(1)

        @pl.when(chip + 3 >= chips)
        def _():
            clear(0)
            clear(1)

        @pl.when(chip + 4 < chips)
        def _():
            far4_copy(cyc, 0).wait_recv()
            decode(2)

            @pl.when(core == 1)
            def _():
                far4_copy(cyc, 1).wait_recv()
                decode(3)

        @pl.when(chip + 4 >= chips)
        def _():
            clear(2)
            clear(3)

        row = lax.broadcasted_iota(jnp.int32, (128, 128), 0)
        lane = lax.broadcasted_iota(jnp.int32, (128, 128), 1)
        inside = lane + row < 128

        def turned(j):
            piece = tiles[cyc, core + j]
            for bit in (1, 2, 4):
                piece = jnp.where(row // bit % 2 == 1, pltpu.roll(piece, 128 - bit, 1), piece)
            return jnp.concatenate(
                [piece[:8]] + [pltpu.roll(piece[r : r + 8], 128 - r, 1) for r in range(8, 128, 8)],
                axis=0,
            )

        now = turned(0)
        for j in range(LAG // 128):
            later = turned(j + 1)
            out[cyc, :, j * 128 : j * 128 + 128] = jnp.where(inside, now, later)
            now = later

    @pl.loop(0, mod_count)
    def _(k):
        @pl.when((k < TRANSIT_LAG) & (k % 2 == 1))
        def _():
            transit(up2, down2, steps - TRANSIT_LAG + k, 9)

        share_stage(k)

    for o in range(mod_count):
        pltpu.make_async_copy(counts.at[o], counts.at[o], count_recv.at[o]).wait()
    compute(0)

    @pl.loop(mod_count, steps)
    def _(k):
        share_stage(k)

    finish(0)
    compute(1)
    finish(1)

    def sent(lane, slot):
        pltpu.make_async_copy(held.at[slot], held.at[slot], send_sem.at[lane]).wait()

    def sent_half(lane, slot):
        part = held.at[slot, pl.ds(0, mod_count)]
        pltpu.make_async_copy(part, part, send_sem.at[lane]).wait()

    @pl.when(first | last)
    def _():
        sent_half(8, up1)
        sent_half(9, up2)

    for cyc in range(2):
        part = held.at[own, pl.ds(cyc * mod_count + 1, mod_count - 1)]
        pltpu.make_async_copy(part, part, send_sem.at[0]).wait()
    for o in range(1, mod_count):
        pltpu.make_async_copy(counts.at[o], counts.at[o], count_send.at[o]).wait()
    for lane, slot, cond in (
        (1, own, has_dn1), (2, own, has_up1), (3, own, None), (4, down1, has_up1 & has_dn1),
        (5, down1, has_up1), (6, up1, has_up1 & has_dn1), (7, down2, has_up2),
    ):
        if cond is None:
            sent(lane, slot)
        else:
            pl.when(cond)(functools.partial(sent, lane, slot))
    for cyc in range(2):
        @pl.when(sends3)
        def _():
            far3_copy(cyc).wait_send()

        @pl.when(sends4)
        def _():
            far4_copy(cyc, 0).wait_send()

            @pl.when(core == 1)
            def _():
                far4_copy(cyc, 1).wait_send()


def shards(frames, cycle_label, good_pixel):
    frame_count, mod_count = lax.axis_size("frame"), lax.axis_size("mod")
    rows, pixels = frames.shape
    steps = 2 * mod_count
    per_cycle = pixels // steps
    small = (pixels // 128, 128)
    return pl.pallas_call(
        functools.partial(kernel, frame_count, mod_count),
        out_shape=jax.ShapeDtypeStruct((2, rows, LAG), jnp.float32),
        in_specs=[pl.BlockSpec(memory_space=pl.ANY)] * 3,
        out_specs=pl.BlockSpec(memory_space=pltpu.VMEM),
        scratch_shapes=[
            pltpu.VMEM((rows, pixels), jnp.bfloat16),
            pltpu.VMEM(small, jnp.int32),
            pltpu.VMEM(small, jnp.int32),
            pltpu.VMEM((pixels, 128), jnp.float32),
            pltpu.VMEM((mod_count, 8, 128), jnp.float32),
            pltpu.VMEM((steps, rows, per_cycle), jnp.bfloat16),
            pltpu.VMEM((10, steps, rows, per_cycle), jnp.bfloat16),
            pltpu.VMEM((mod_count, 8, 128), jnp.float32),
            pltpu.VMEM((2, 10, 128, 128), jnp.float32),
            pltpu.VMEM((2, 4, 128, 128), jnp.int16),
            pltpu.VMEM((2, 4, 128, 128), jnp.int16),
            pltpu.SemaphoreType.DMA((3,)),
            pltpu.SemaphoreType.DMA((10, steps)),
            pltpu.SemaphoreType.DMA((10,)),
            pltpu.SemaphoreType.DMA((mod_count,)),
            pltpu.SemaphoreType.DMA((mod_count,)),
            pltpu.SemaphoreType.DMA((2, 3)),
            pltpu.SemaphoreType.DMA((2, 3)),
        ],
        compiler_params=pltpu.CompilerParams(
            collective_id=0, has_side_effects=True, vmem_limit_bytes=32 * 1024 * 1024
        ),
    )(pltpu.with_memory_space_constraint(frames, pltpu.HBM), cycle_label.reshape(small), good_pixel.reshape(small))


def solution(mesh):
    placed = (P("frame", "mod"), P("mod"), P("mod"))
    return jax.shard_map(
        shards, mesh=mesh, in_specs=placed, out_specs=P("mod", "frame", None), check_vma=False
    )
```

```python
import functools

import jax
import jax.numpy as jnp
from jax import lax
from jax.experimental import pallas as pl
from jax.experimental.pallas import tpu as pltpu
from jax.sharding import PartitionSpec as P

CYCLES = 16
LAG = 1024
MESH = pl.DeviceIdType.MESH
TRANSIT_LAG = 2
OWN_LAG = 6
RELAY_LAG = 6
CODE = 5600.0
NT = (((1,), (1,)), ((), ()))


def nt_dot(a, b):
    return lax.dot_general(a, b, NT, preferred_element_type=jnp.float32)


def rank_pixels(label_ref, good_ref, place, partial, cycles, per_cycle):
    rows, lanes = label_ref.shape
    label = label_ref[...]
    good = good_ref[...] > 0
    member = jnp.concatenate([jnp.where(label == c, 1.0, 0.0) for c in range(cycles)], axis=0)
    before = lax.broadcasted_iota(jnp.int32, (lanes, lanes), 0)
    at = lax.broadcasted_iota(jnp.int32, (lanes, lanes), 1)
    upper = jnp.where(before < at, 1.0, 0.0).astype(jnp.bfloat16)
    ones = jnp.ones((lanes, lanes), jnp.bfloat16)
    packed = member.astype(jnp.bfloat16)
    in_row = jnp.dot(packed, upper, preferred_element_type=jnp.float32)
    totals = jnp.dot(packed, ones, preferred_element_type=jnp.float32).astype(jnp.bfloat16)
    side = jnp.concatenate([totals[c * rows : (c + 1) * rows] for c in range(cycles)], axis=1)
    here = lax.broadcasted_iota(jnp.int32, (rows, rows), 0)
    there = lax.broadcasted_iota(jnp.int32, (rows, rows), 1)
    earlier = jnp.where(there < here, 1.0, 0.0).astype(jnp.bfloat16)
    above = jnp.dot(earlier, side, preferred_element_type=jnp.float32)
    usable = jnp.where(good, 1.0, 0.0)
    partial[...] = jnp.zeros_like(partial)
    total = None
    for c in range(cycles):
        mine = slice(c * rows, (c + 1) * rows)
        ranks = (in_row[mine] + above[:, c * lanes : (c + 1) * lanes]) * member[mine]
        total = ranks if total is None else total + ranks
        per_row = jnp.sum(member[mine] * usable, axis=0, keepdims=True)
        partial[c // 2, c % 2 : c % 2 + 1, :] = jnp.broadcast_to(
            jnp.sum(per_row, axis=1, keepdims=True), (1, lanes)
        )
    where = jnp.where(good, total + label.astype(jnp.float32) * per_cycle, -1.0)
    for r in range(rows):
        place[r * lanes : (r + 1) * lanes, :] = jnp.broadcast_to(where[r : r + 1], (lanes, lanes)).T


def kernel(
    frame_count, mod_count, frames_hbm, label_hbm, good_hbm, out,
    frames, label, good, place, partial, packed, held, counts, tiles, far, code, gram, sums,
    in_sem, recv_sem, send_sem, count_send, count_recv, far_send, far_recv,
):
    f = lax.axis_index("frame")
    m = lax.axis_index("mod")
    core = f % 2
    chip = f // 2
    chips = frame_count // 2
    y_count = mod_count // 2
    y, x = m // 2, m % 2
    partner = f + 1 - 2 * core
    steps = 2 * mod_count
    cycles = 2 * mod_count
    rows, per_cycle = packed.shape[1:]

    has_up1, has_up2 = chip + 1 < chips, chip + 2 < chips
    has_dn1, has_dn2 = chip >= 1, chip >= 2

    own, down1, down2, up1, up2 = 4 + core, 6 + core, 8 + core, 2 + core, core
    other_down1, other_down2, other_own = 7 - core, 9 - core, 5 - core

    loads = [
        pltpu.make_async_copy(src, dst, in_sem.at[i])
        for i, (src, dst) in enumerate(
            ((label_hbm, label), (good_hbm, good), (frames_hbm, frames))
        )
    ]
    for load in loads:
        load.start()

    half = chips // 2
    first, last = chip == 0, chip == chips - 1
    below, above = chip == half - 1, chip == half
    at_first, at_last = core, frame_count - 2 + core
    at_below, at_above = 2 * half - 2 + core, 2 * half + core

    def peer(o, sign):
        dy, dx = o // 2, o % 2
        return ((y + sign * dy + y_count) % y_count) * 2 + (x + dx) % 2

    barrier = pltpu.get_barrier_semaphore()

    def greet(cond, fr, mo):
        @pl.when(cond)
        def _():
            pl.semaphore_signal(barrier, inc=1, device_id=(fr, mo), device_id_type=MESH)

    for o in range(1, mod_count):
        pl.semaphore_signal(barrier, inc=1, device_id=(f, peer(o, 1)), device_id_type=MESH)
    pl.semaphore_signal(barrier, inc=1, device_id=(partner, m), device_id_type=MESH)
    greet(has_up1, f + 2, m)
    greet(has_up2, f + 4, m)
    greet(has_dn1, f - 2, m)
    greet(has_dn2, f - 4, m)
    for ends, targets in (
        (first | last, (at_below, at_above)), (below | above, (at_first, at_last))
    ):
        for target in targets:
            greet(ends, target, m)
    arrivals = mod_count
    ends = first | last | below | above
    for cond in (has_up1, has_up2, has_dn1, has_dn2, ends, ends):
        arrivals = arrivals + jnp.where(cond, 1, 0)

    loads[0].wait()
    loads[1].wait()
    rank_pixels(label, good, place, partial, cycles, per_cycle)
    loads[2].wait()
    pl.semaphore_wait(barrier, arrivals)

    def remote(src, dst, send, recv, fr, mo):
        return pltpu.make_async_remote_copy(
            src_ref=src, dst_ref=dst, send_sem=send, recv_sem=recv,
            device_id=(fr, mo), device_id_type=MESH,
        )

    def forward(from_slot, to_slot, k, lane, fr):
        source = packed.at[k] if from_slot is None else held.at[from_slot, k]
        remote(
            source, held.at[to_slot, k], send_sem.at[lane],
            recv_sem.at[to_slot, k], fr, m,
        ).start()

    def arrived(slot, k):
        pltpu.make_async_copy(held.at[slot, k], held.at[slot, k], recv_sem.at[slot, k]).wait()

    def arrange(k):
        cyc, o = k // mod_count, k % mod_count
        cycle = 2 * peer(o, -1) + cyc
        lane = lax.broadcasted_iota(jnp.int32, (256, 128), 1) + cycle * per_cycle
        wanted = [(lane + h * 128).astype(jnp.float32) for h in range(per_cycle // 128)]
        total = None
        for r in range(0, frames.shape[1], 256):
            spot = place[r : r + 256, :]
            hot = jnp.concatenate(
                [jnp.where(spot == w, 1.0, 0.0).astype(jnp.bfloat16) for w in wanted], axis=1
            )
            term = jnp.dot(frames[:, r : r + 256], hot, preferred_element_type=jnp.float32)
            total = term if total is None else total + term
        packed[k] = total.astype(jnp.bfloat16)

    def launch(k):
        o = k % mod_count

        @pl.when(o == 0)
        def _():
            pltpu.make_async_copy(packed.at[k], held.at[own, k], recv_sem.at[own, k]).start()

        @pl.when(o > 0)
        def _():
            remote(
                packed.at[k], held.at[own, k], send_sem.at[0], recv_sem.at[own, k], f, peer(o, -1)
            ).start()

    def forward_down(from_slot, to_slot, by_slot, k, lane):
        detour = above & (k % 2 == 1)

        @pl.when(detour)
        def _():
            forward(from_slot, by_slot, k, lane, at_first)

        @pl.when(has_dn1 & jnp.logical_not(detour))
        def _():
            forward(from_slot, to_slot, k, lane, f - 2)

    def forward_up(from_slot, to_slot, by_slot, k, lane):
        detour = below & (k % 2 == 1)

        @pl.when(detour)
        def _():
            forward(from_slot, by_slot, k, lane, at_last)

        @pl.when(has_up1 & jnp.logical_not(detour))
        def _():
            forward(from_slot, to_slot, k, lane, f + 2)

    def transit(up_slot, down_slot, k, lane):
        @pl.when(first)
        def _():
            arrived(up_slot, k)
            forward(up_slot, down_slot, k, lane, at_below)

        @pl.when(last)
        def _():
            arrived(down_slot, k)
            forward(down_slot, up_slot, k, lane, at_above)

    def own_stage(k, source):
        forward_down(source, down1, up1, k, 1)
        forward_up(source, up1, down1, k, 2)
        forward(source, own, k, 3, partner)

    def relay_stage(k):
        @pl.when(has_up1)
        def _():
            arrived(down1, k)
            forward_down(down1, down2, up2, k, 4)
            forward(down1, down1, k, 5, partner)

        @pl.when(has_dn1)
        def _():
            arrived(up1, k)
            forward_up(up1, up2, down2, k, 6)

    def share_stage(k):
        @pl.when(has_up2)
        def _():
            arrived(down2, k)
            forward(down2, down2, k, 7, partner)

    for o in range(mod_count):
        to = peer(o, -1)
        if o == 0:
            pltpu.make_async_copy(partial.at[to], counts.at[o], count_recv.at[o]).start()
        else:
            remote(partial.at[to], counts.at[o], count_send.at[o], count_recv.at[o], f, to).start()

    def slab(i):
        early = jnp.where(i == 1, mod_count, i - 1)
        return jnp.where((i >= 1) & (i <= mod_count), early, i)

    @pl.loop(0, steps + OWN_LAG + RELAY_LAG + TRANSIT_LAG)
    def _(i):
        @pl.when(i < steps)
        def _():
            arrange(slab(i))

        @pl.when((i >= 1) & (i <= steps))
        def _():
            launch(slab(i - 1))

        @pl.when((i >= 1) & (i < 3))
        def _():
            own_stage(slab(i - 1), None)

        @pl.when((i >= OWN_LAG + 2) & (i < steps + OWN_LAG))
        def _():
            arrived(own, slab(i - OWN_LAG))
            own_stage(slab(i - OWN_LAG), own)

        passed = slab(i - OWN_LAG - TRANSIT_LAG)

        @pl.when((i >= OWN_LAG + TRANSIT_LAG) & (passed < steps) & (passed % 2 == 1))
        def _():
            transit(up1, down1, passed, 8)

        relayed = i - OWN_LAG - RELAY_LAG

        @pl.when((relayed >= 0) & (relayed < steps))
        def _():
            relay_stage(slab(relayed))

        passed_on = slab(relayed - TRANSIT_LAG)

        @pl.when((relayed >= TRANSIT_LAG) & (passed_on % 2 == 1))
        def _():
            transit(up2, down2, passed_on, 9)

    def far3_copy(cyc):
        return remote(
            far.at[cyc, pl.ds(0, 2)], code.at[cyc, pl.ds(0, 2)],
            far_send.at[cyc, 0], far_recv.at[cyc, 0], f - 2, m,
        )

    def far4_copy(cyc, i):
        return remote(
            far.at[cyc, 2 + i], code.at[cyc, 2 + i],
            far_send.at[cyc, 1 + i], far_recv.at[cyc, 1 + i], f - 4, m,
        )

    sends3, sends4 = has_dn1 & has_up2, has_dn2 & has_up2

    everything = range(mod_count)

    def products(cyc, lhs_slots, rhs_slot, span):
        ones = jnp.ones((16, per_cycle), jnp.bfloat16)
        total = None
        for o in span:
            k = cyc * mod_count + o
            lhs = jnp.concatenate([held[s, k] for s in lhs_slots] + [ones], axis=0)
            rhs = held[rhs_slot : rhs_slot + 2, k].reshape(2 * rows, per_cycle)
            term = nt_dot(lhs, rhs)
            total = term if total is None else total + term
        return total

    def row_sums(cyc, slot, span):
        total = None
        for o in span:
            block = held[slot, cyc * mod_count + o].astype(jnp.float32)
            total = block if total is None else total + block
        return jnp.broadcast_to(jnp.sum(total, axis=1, keepdims=True), (rows, 128))

    def cycle_count(cyc):
        count = counts[0]
        for o in range(1, mod_count):
            count = count + counts[o]
        return count[cyc : cyc + 1]

    def correlated(total, i, earlier, later, side, count):
        span = slice(side * 128, side * 128 + 128)
        return total[i * 128 : i * 128 + 128, span] * count / (earlier * later[:, span])

    def near(cyc):
        @pl.loop(0, mod_count)
        def _(o):
            k = cyc * mod_count + o
            arrived(other_own, k)

            @pl.when(has_up1)
            def _():
                arrived(other_down1, k)

        arrived(own, cyc * mod_count)
        count = cycle_count(cyc)
        mine = row_sums(cyc, own, everything)
        sums[cyc, 0] = mine

        @pl.when(has_dn1)
        def _():
            sums[cyc, 1] = row_sums(cyc, up1, everything)

        def part(rhs_slot):
            total = products(cyc, (own,), rhs_slot, everything)
            for side in range(2):
                tiles[cyc, rhs_slot - 4 + side] = correlated(
                    total, 0, mine, total[rows : rows + 1], side, count
                )

        part(4)

        @pl.when(has_up1)
        def _():
            part(6)

        @pl.when(jnp.logical_not(has_up1))
        def _():
            tiles[cyc, 2:4] = jnp.zeros((2, 128, 128), jnp.float32)

        blocks(cyc, 0, 2)

    def gather_far(cyc, start, stop):
        @pl.loop(start, stop)
        def _(o):
            k = cyc * mod_count + o

            @pl.when(has_up2)
            def _():
                arrived(other_down2, k)

            @pl.when(has_dn2)
            def _():
                arrived(up2, k)

        @pl.when(has_up2)
        def _():
            span = range(start, stop)
            total = products(cyc, (up1, up2, own), 8, span)
            second = row_sums(cyc, up2, span)
            if start > 0:
                total, second = total + gram[...], second + sums[cyc, 2]
            gram[...] = total
            sums[cyc, 2] = second

    def far_tiles(cyc):
        @pl.when(has_up2)
        def _():
            count = cycle_count(cyc)
            total = gram[...]
            later = total[3 * rows : 3 * rows + 1]

            def coded(i):
                for side in range(2):
                    value = correlated(total, i, sums[cyc, 1 + i], later, side, count)
                    far[cyc, 2 * i + side] = (
                        jnp.round(jnp.log(value) * CODE).astype(jnp.int32).astype(jnp.int16)
                    )

            coded(1)
            coded(0)
            for side in range(2):
                tiles[cyc, 4 + side] = correlated(total, 2, sums[cyc, 0], later, side, count)

        @pl.when(sends4)
        def _():
            far4_copy(cyc, 0).start()

            @pl.when(core == 1)
            def _():
                far4_copy(cyc, 1).start()

        @pl.when(sends3)
        def _():
            far3_copy(cyc).start()

        @pl.when(jnp.logical_not(has_up2))
        def _():
            tiles[cyc, 4:6] = jnp.zeros((2, 128, 128), jnp.float32)

    def finish(cyc):
        def decode(i):
            value = code[cyc, i].astype(jnp.int32).astype(jnp.float32)
            tiles[cyc, 6 + i] = jnp.exp(value * (1.0 / CODE))

        def clear(i):
            tiles[cyc, 6 + i] = jnp.zeros((128, 128), jnp.float32)

        @pl.when(chip + 3 < chips)
        def _():
            far3_copy(cyc).wait_recv()
            decode(0)
            decode(1)

        @pl.when(chip + 3 >= chips)
        def _():
            clear(0)
            clear(1)

        @pl.when(chip + 4 < chips)
        def _():
            far4_copy(cyc, 0).wait_recv()
            decode(2)

            @pl.when(core == 1)
            def _():
                far4_copy(cyc, 1).wait_recv()
                decode(3)

        @pl.when(chip + 4 >= chips)
        def _():
            clear(2)
            clear(3)

        blocks(cyc, 2, LAG // 128)

    def blocks(cyc, start, stop):
        row = lax.broadcasted_iota(jnp.int32, (128, 128), 0)
        lane = lax.broadcasted_iota(jnp.int32, (128, 128), 1)
        inside = lane + row < 128

        def turned(j):
            piece = tiles[cyc, core + j]
            for bit in (1, 2, 4):
                piece = jnp.where(row // bit % 2 == 1, pltpu.roll(piece, 128 - bit, 1), piece)
            return jnp.concatenate(
                [piece[:8]] + [pltpu.roll(piece[r : r + 8], 128 - r, 1) for r in range(8, 128, 8)],
                axis=0,
            )

        now = turned(start)
        for j in range(start, stop):
            later = turned(j + 1)
            out[cyc, :, j * 128 : j * 128 + 128] = jnp.where(inside, now, later)
            now = later

    for o in range(mod_count):
        pltpu.make_async_copy(counts.at[o], counts.at[o], count_recv.at[o]).wait()
    near(0)
    near(1)

    def share(start, stop):
        @pl.loop(start, stop)
        def _(k):
            share_stage(k)

    share(0, mod_count)
    gather_far(0, 0, mod_count)
    far_tiles(0)
    split = max(1, mod_count - 2)
    share(mod_count, mod_count + split)
    gather_far(1, 0, split)
    share(mod_count + split, steps)
    gather_far(1, split, mod_count)
    far_tiles(1)
    finish(0)
    finish(1)

    def sent(lane, slot):
        pltpu.make_async_copy(held.at[slot], held.at[slot], send_sem.at[lane]).wait()

    def sent_half(lane, slot):
        part = held.at[slot, pl.ds(0, mod_count)]
        pltpu.make_async_copy(part, part, send_sem.at[lane]).wait()

    @pl.when(first | last)
    def _():
        sent_half(8, up1)
        sent_half(9, up2)

    for cyc in range(2):
        part = held.at[own, pl.ds(cyc * mod_count + 1, mod_count - 1)]
        pltpu.make_async_copy(part, part, send_sem.at[0]).wait()
    for o in range(1, mod_count):
        pltpu.make_async_copy(counts.at[o], counts.at[o], count_send.at[o]).wait()
    for lane, slot, cond in (
        (1, own, has_dn1), (2, own, has_up1), (3, own, None), (4, down1, has_up1 & has_dn1),
        (5, down1, has_up1), (6, up1, has_up1 & has_dn1), (7, down2, has_up2),
    ):
        if cond is None:
            sent(lane, slot)
        else:
            pl.when(cond)(functools.partial(sent, lane, slot))
    for cyc in range(2):
        @pl.when(sends3)
        def _():
            far3_copy(cyc).wait_send()

        @pl.when(sends4)
        def _():
            far4_copy(cyc, 0).wait_send()

            @pl.when(core == 1)
            def _():
                far4_copy(cyc, 1).wait_send()


def shards(frames, cycle_label, good_pixel):
    frame_count, mod_count = lax.axis_size("frame"), lax.axis_size("mod")
    rows, pixels = frames.shape
    steps = 2 * mod_count
    per_cycle = pixels // steps
    small = (pixels // 128, 128)
    return pl.pallas_call(
        functools.partial(kernel, frame_count, mod_count),
        out_shape=jax.ShapeDtypeStruct((2, rows, LAG), jnp.float32),
        in_specs=[pl.BlockSpec(memory_space=pl.ANY)] * 3,
        out_specs=pl.BlockSpec(memory_space=pltpu.VMEM),
        scratch_shapes=[
            pltpu.VMEM((rows, pixels), jnp.bfloat16),
            pltpu.VMEM(small, jnp.int32),
            pltpu.VMEM(small, jnp.int32),
            pltpu.VMEM((pixels, 128), jnp.float32),
            pltpu.VMEM((mod_count, 8, 128), jnp.float32),
            pltpu.VMEM((steps, rows, per_cycle), jnp.bfloat16),
            pltpu.VMEM((10, steps, rows, per_cycle), jnp.bfloat16),
            pltpu.VMEM((mod_count, 8, 128), jnp.float32),
            pltpu.VMEM((2, 10, 128, 128), jnp.float32),
            pltpu.VMEM((2, 4, 128, 128), jnp.int16),
            pltpu.VMEM((2, 4, 128, 128), jnp.int16),
            pltpu.VMEM((3 * rows + 16, 256), jnp.float32),
            pltpu.VMEM((2, 3, 128, 128), jnp.float32),
            pltpu.SemaphoreType.DMA((3,)),
            pltpu.SemaphoreType.DMA((10, steps)),
            pltpu.SemaphoreType.DMA((10,)),
            pltpu.SemaphoreType.DMA((mod_count,)),
            pltpu.SemaphoreType.DMA((mod_count,)),
            pltpu.SemaphoreType.DMA((2, 3)),
            pltpu.SemaphoreType.DMA((2, 3)),
        ],
        compiler_params=pltpu.CompilerParams(
            collective_id=0, has_side_effects=True, vmem_limit_bytes=32 * 1024 * 1024
        ),
    )(pltpu.with_memory_space_constraint(frames, pltpu.HBM), cycle_label.reshape(small), good_pixel.reshape(small))


def solution(mesh):
    placed = (P("frame", "mod"), P("mod"), P("mod"))
    return jax.shard_map(
        shards, mesh=mesh, in_specs=placed, out_specs=P("mod", "frame", None), check_vma=False
    )
```

```python
import functools

import jax
import jax.numpy as jnp
from jax import lax
from jax.experimental import pallas as pl
from jax.experimental.pallas import tpu as pltpu
from jax.sharding import PartitionSpec as P

CYCLES = 16
LAG = 1024
MESH = pl.DeviceIdType.MESH
TRANSIT_LAG = 2
OWN_LAG = 6
RELAY_LAG = 6
CODE = 5600.0
NT = (((1,), (1,)), ((), ()))


def nt_dot(a, b):
    return lax.dot_general(a, b, NT, preferred_element_type=jnp.float32)


def rank_pixels(label_ref, good_ref, place, partial, cycles, per_cycle):
    rows, lanes = label_ref.shape
    label = label_ref[...]
    good = good_ref[...] > 0
    member = jnp.concatenate([jnp.where(label == c, 1.0, 0.0) for c in range(cycles)], axis=0)
    before = lax.broadcasted_iota(jnp.int32, (lanes, lanes), 0)
    at = lax.broadcasted_iota(jnp.int32, (lanes, lanes), 1)
    upper = jnp.where(before < at, 1.0, 0.0).astype(jnp.bfloat16)
    ones = jnp.ones((lanes, lanes), jnp.bfloat16)
    packed = member.astype(jnp.bfloat16)
    in_row = jnp.dot(packed, upper, preferred_element_type=jnp.float32)
    totals = jnp.dot(packed, ones, preferred_element_type=jnp.float32).astype(jnp.bfloat16)
    side = jnp.concatenate([totals[c * rows : (c + 1) * rows] for c in range(cycles)], axis=1)
    here = lax.broadcasted_iota(jnp.int32, (rows, rows), 0)
    there = lax.broadcasted_iota(jnp.int32, (rows, rows), 1)
    earlier = jnp.where(there < here, 1.0, 0.0).astype(jnp.bfloat16)
    above = jnp.dot(earlier, side, preferred_element_type=jnp.float32)
    usable = jnp.where(good, 1.0, 0.0)
    partial[...] = jnp.zeros_like(partial)
    total = None
    for c in range(cycles):
        mine = slice(c * rows, (c + 1) * rows)
        ranks = (in_row[mine] + above[:, c * lanes : (c + 1) * lanes]) * member[mine]
        total = ranks if total is None else total + ranks
        per_row = jnp.sum(member[mine] * usable, axis=0, keepdims=True)
        partial[c // 2, c % 2 : c % 2 + 1, :] = jnp.broadcast_to(
            jnp.sum(per_row, axis=1, keepdims=True), (1, lanes)
        )
    where = jnp.where(good, total + label.astype(jnp.float32) * per_cycle, -1.0)
    for r in range(rows):
        place[r * lanes : (r + 1) * lanes, :] = jnp.broadcast_to(where[r : r + 1], (lanes, lanes)).T


def kernel(
    frame_count, mod_count, frames_hbm, label_hbm, good_hbm, out,
    frames, label, good, place, partial, packed, held, counts, tiles, far, code, corner, corner_code, gram, sums,
    in_sem, recv_sem, send_sem, count_send, count_recv, far_send, far_recv,
):
    f = lax.axis_index("frame")
    m = lax.axis_index("mod")
    core = f % 2
    chip = f // 2
    chips = frame_count // 2
    y_count = mod_count // 2
    y, x = m // 2, m % 2
    partner = f + 1 - 2 * core
    steps = 2 * mod_count
    cycles = 2 * mod_count
    rows, per_cycle = packed.shape[1:]

    has_up1, has_up2 = chip + 1 < chips, chip + 2 < chips
    has_dn1, has_dn2 = chip >= 1, chip >= 2

    own, down1, down2, up1, up2 = 4 + core, 6 + core, 8 + core, 2 + core, core
    other_down1, other_down2, other_own = 7 - core, 9 - core, 5 - core

    loads = [
        pltpu.make_async_copy(src, dst, in_sem.at[i])
        for i, (src, dst) in enumerate(
            ((label_hbm, label), (good_hbm, good), (frames_hbm, frames))
        )
    ]
    for load in loads:
        load.start()

    half = chips // 2
    first, last = chip == 0, chip == chips - 1
    below, above = chip == half - 1, chip == half
    at_first, at_last = core, frame_count - 2 + core
    at_below, at_above = 2 * half - 2 + core, 2 * half + core

    def peer(o, sign):
        dy, dx = o // 2, o % 2
        return ((y + sign * dy + y_count) % y_count) * 2 + (x + dx) % 2

    barrier = pltpu.get_barrier_semaphore()

    def greet(cond, fr, mo):
        @pl.when(cond)
        def _():
            pl.semaphore_signal(barrier, inc=1, device_id=(fr, mo), device_id_type=MESH)

    for o in range(1, mod_count):
        pl.semaphore_signal(barrier, inc=1, device_id=(f, peer(o, 1)), device_id_type=MESH)
    pl.semaphore_signal(barrier, inc=1, device_id=(partner, m), device_id_type=MESH)
    greet(has_up1, f + 2, m)
    greet(has_up2, f + 4, m)
    greet(has_dn1, f - 2, m)
    greet(has_dn2, f - 4, m)
    for ends, targets in (
        (first | last, (at_below, at_above)), (below | above, (at_first, at_last))
    ):
        for target in targets:
            greet(ends, target, m)
    arrivals = mod_count
    ends = first | last | below | above
    for cond in (has_up1, has_up2, has_dn1, has_dn2, ends, ends):
        arrivals = arrivals + jnp.where(cond, 1, 0)

    loads[0].wait()
    loads[1].wait()
    rank_pixels(label, good, place, partial, cycles, per_cycle)
    loads[2].wait()
    pl.semaphore_wait(barrier, arrivals)

    def remote(src, dst, send, recv, fr, mo):
        return pltpu.make_async_remote_copy(
            src_ref=src, dst_ref=dst, send_sem=send, recv_sem=recv,
            device_id=(fr, mo), device_id_type=MESH,
        )

    def forward(from_slot, to_slot, k, lane, fr):
        source = packed.at[k] if from_slot is None else held.at[from_slot, k]
        remote(
            source, held.at[to_slot, k], send_sem.at[lane],
            recv_sem.at[to_slot, k], fr, m,
        ).start()

    def arrived(slot, k):
        pltpu.make_async_copy(held.at[slot, k], held.at[slot, k], recv_sem.at[slot, k]).wait()

    def arrange(k):
        cyc, o = k // mod_count, k % mod_count
        cycle = 2 * peer(o, -1) + cyc
        lane = lax.broadcasted_iota(jnp.int32, (256, 128), 1) + cycle * per_cycle
        wanted = [(lane + h * 128).astype(jnp.float32) for h in range(per_cycle // 128)]
        total = None
        for r in range(0, frames.shape[1], 256):
            spot = place[r : r + 256, :]
            hot = jnp.concatenate(
                [jnp.where(spot == w, 1.0, 0.0).astype(jnp.bfloat16) for w in wanted], axis=1
            )
            term = jnp.dot(frames[:, r : r + 256], hot, preferred_element_type=jnp.float32)
            total = term if total is None else total + term
        packed[k] = total.astype(jnp.bfloat16)

    def launch(k):
        o = k % mod_count

        @pl.when(o == 0)
        def _():
            pltpu.make_async_copy(packed.at[k], held.at[own, k], recv_sem.at[own, k]).start()

        @pl.when(o > 0)
        def _():
            remote(
                packed.at[k], held.at[own, k], send_sem.at[0], recv_sem.at[own, k], f, peer(o, -1)
            ).start()

    def forward_down(from_slot, to_slot, by_slot, k, lane):
        detour = above & (k % 2 == 1)

        @pl.when(detour)
        def _():
            forward(from_slot, by_slot, k, lane, at_first)

        @pl.when(has_dn1 & jnp.logical_not(detour))
        def _():
            forward(from_slot, to_slot, k, lane, f - 2)

    def forward_up(from_slot, to_slot, by_slot, k, lane):
        detour = below & (k % 2 == 1)

        @pl.when(detour)
        def _():
            forward(from_slot, by_slot, k, lane, at_last)

        @pl.when(has_up1 & jnp.logical_not(detour))
        def _():
            forward(from_slot, to_slot, k, lane, f + 2)

    def transit(up_slot, down_slot, k, lane):
        @pl.when(first)
        def _():
            arrived(up_slot, k)
            forward(up_slot, down_slot, k, lane, at_below)

        @pl.when(last)
        def _():
            arrived(down_slot, k)
            forward(down_slot, up_slot, k, lane, at_above)

    def own_stage(k, source):
        forward_down(source, down1, up1, k, 1)
        forward_up(source, up1, down1, k, 2)
        forward(source, own, k, 3, partner)

    def relay_stage(k):
        @pl.when(has_up1)
        def _():
            arrived(down1, k)
            forward_down(down1, down2, up2, k, 4)
            forward(down1, down1, k, 5, partner)

        @pl.when(has_dn1)
        def _():
            arrived(up1, k)
            forward_up(up1, up2, down2, k, 6)

    def share_stage(k):
        @pl.when(has_up2)
        def _():
            arrived(down2, k)
            forward(down2, down2, k, 7, partner)

    for o in range(mod_count):
        to = peer(o, -1)
        if o == 0:
            pltpu.make_async_copy(partial.at[to], counts.at[o], count_recv.at[o]).start()
        else:
            remote(partial.at[to], counts.at[o], count_send.at[o], count_recv.at[o], f, to).start()

    def slab(i):
        early = jnp.where(i == 1, mod_count, i - 1)
        return jnp.where((i >= 1) & (i <= mod_count), early, i)

    @pl.loop(0, steps + OWN_LAG + RELAY_LAG + TRANSIT_LAG)
    def _(i):
        @pl.when(i < steps)
        def _():
            arrange(slab(i))

        @pl.when((i >= 1) & (i <= steps))
        def _():
            launch(slab(i - 1))

        @pl.when((i >= 1) & (i < 3))
        def _():
            own_stage(slab(i - 1), None)

        @pl.when((i >= OWN_LAG + 2) & (i < steps + OWN_LAG))
        def _():
            arrived(own, slab(i - OWN_LAG))
            own_stage(slab(i - OWN_LAG), own)

        passed = slab(i - OWN_LAG - TRANSIT_LAG)

        @pl.when((i >= OWN_LAG + TRANSIT_LAG) & (passed < steps) & (passed % 2 == 1))
        def _():
            transit(up1, down1, passed, 8)

        relayed = i - OWN_LAG - RELAY_LAG

        @pl.when((relayed >= 0) & (relayed < steps))
        def _():
            relay_stage(slab(relayed))

        passed_on = slab(relayed - TRANSIT_LAG)

        @pl.when((relayed >= TRANSIT_LAG) & (passed_on % 2 == 1))
        def _():
            transit(up2, down2, passed_on, 9)

    def far3_copy(cyc):
        return remote(
            far.at[cyc, pl.ds(0, 2)], code.at[cyc, pl.ds(0, 2)],
            far_send.at[cyc, 0], far_recv.at[cyc, 0], f - 2, m,
        )

    def far4_copy(cyc, i):
        source, target = (far, code) if i else (corner, corner_code)
        place_of = (cyc, 2) if i else (cyc,)
        return remote(
            source.at[place_of], target.at[place_of],
            far_send.at[cyc, 1 + i], far_recv.at[cyc, 1 + i], f - 4, m,
        )

    def folded(tile):
        lane = lax.broadcasted_iota(jnp.int32, (8, 128), 1)
        parts = [
            jnp.where(
                lane < 8 * g + 8,
                tile[8 * g : 8 * g + 8],
                pltpu.roll(tile[112 - 8 * g : 120 - 8 * g], 8 * g + 8, 1),
            )
            for g in range(8, 15)
        ]
        return jnp.concatenate(parts + [tile[120:], tile[56:64], tile[56:64]], axis=0)

    def unfolded(tile):
        parts = [
            pltpu.roll(tile[8 * (6 - h) : 8 * (6 - h) + 8], 8 * h + 8, 1) for h in range(7)
        ]
        return jnp.concatenate(parts + [tile[64:72], tile[:56], tile[56:64]], axis=0)

    sends3, sends4 = has_dn1 & has_up2, has_dn2 & has_up2

    everything = range(mod_count)

    def products(cyc, lhs_slots, rhs_slot, span):
        ones = jnp.ones((16, per_cycle), jnp.bfloat16)
        total = None
        for o in span:
            k = cyc * mod_count + o
            lhs = jnp.concatenate([held[s, k] for s in lhs_slots] + [ones], axis=0)
            rhs = held[rhs_slot : rhs_slot + 2, k].reshape(2 * rows, per_cycle)
            term = nt_dot(lhs, rhs)
            total = term if total is None else total + term
        return total

    def row_sums(cyc, slot, span):
        total = None
        for o in span:
            block = held[slot, cyc * mod_count + o].astype(jnp.float32)
            total = block if total is None else total + block
        return jnp.broadcast_to(jnp.sum(total, axis=1, keepdims=True), (rows, 128))

    def cycle_count(cyc):
        count = counts[0]
        for o in range(1, mod_count):
            count = count + counts[o]
        return count[cyc : cyc + 1]

    def correlated(total, i, earlier, later, side, count):
        span = slice(side * 128, side * 128 + 128)
        return total[i * 128 : i * 128 + 128, span] * count / (earlier * later[:, span])

    def near(cyc):
        @pl.loop(0, mod_count)
        def _(o):
            k = cyc * mod_count + o
            arrived(other_own, k)

            @pl.when(has_up1)
            def _():
                arrived(other_down1, k)

        arrived(own, cyc * mod_count)
        count = cycle_count(cyc)
        mine = row_sums(cyc, own, everything)
        sums[cyc, 0] = mine

        @pl.when(has_dn1)
        def _():
            sums[cyc, 1] = row_sums(cyc, up1, everything)

        def part(rhs_slot):
            total = products(cyc, (own,), rhs_slot, everything)
            for side in range(2):
                tiles[cyc, rhs_slot - 4 + side] = correlated(
                    total, 0, mine, total[rows : rows + 1], side, count
                )

        part(4)

        @pl.when(has_up1)
        def _():
            part(6)

        @pl.when(jnp.logical_not(has_up1))
        def _():
            tiles[cyc, 2:4] = jnp.zeros((2, 128, 128), jnp.float32)

        blocks(cyc, 0, 2)

    def gather_far(cyc, start, stop):
        @pl.loop(start, stop)
        def _(o):
            k = cyc * mod_count + o

            @pl.when(has_up2)
            def _():
                arrived(other_down2, k)

            @pl.when(has_dn2)
            def _():
                arrived(up2, k)

        @pl.when(has_up2)
        def _():
            span = range(start, stop)
            total = products(cyc, (up1, up2, own), 8, span)
            second = row_sums(cyc, up2, span)
            if start > 0:
                total, second = total + gram[...], second + sums[cyc, 2]
            gram[...] = total
            sums[cyc, 2] = second

    def far_tiles(cyc):
        @pl.when(has_up2)
        def _():
            count = cycle_count(cyc)
            total = gram[...]
            later = total[3 * rows : 3 * rows + 1]

            def coded(i, side):
                value = correlated(total, i, sums[cyc, 1 + i], later, side, count)
                return jnp.round(jnp.log(value) * CODE).astype(jnp.int32)

            near_side, far_side = coded(1, 0), coded(1, 1)
            far[cyc, 2] = near_side.astype(jnp.int16)
            corner[cyc] = folded(jnp.where(core == 0, near_side, far_side)).astype(jnp.int16)
            for side in range(2):
                far[cyc, side] = coded(0, side).astype(jnp.int16)
            for side in range(2):
                tiles[cyc, 4 + side] = correlated(total, 2, sums[cyc, 0], later, side, count)

        @pl.when(sends4)
        def _():
            far4_copy(cyc, 0).start()

            @pl.when(core == 1)
            def _():
                far4_copy(cyc, 1).start()

        @pl.when(sends3)
        def _():
            far3_copy(cyc).start()

        @pl.when(jnp.logical_not(has_up2))
        def _():
            tiles[cyc, 4:6] = jnp.zeros((2, 128, 128), jnp.float32)

    def finish(cyc):
        def decode(i):
            value = code[cyc, i].astype(jnp.int32).astype(jnp.float32)
            tiles[cyc, 6 + i] = jnp.exp(value * (1.0 / CODE))

        def clear(i):
            tiles[cyc, 6 + i] = jnp.zeros((128, 128), jnp.float32)

        @pl.when(chip + 3 < chips)
        def _():
            far3_copy(cyc).wait_recv()
            decode(0)
            decode(1)

        @pl.when(chip + 3 >= chips)
        def _():
            clear(0)
            clear(1)

        @pl.when(chip + 4 < chips)
        def _():
            far4_copy(cyc, 0).wait_recv()
            value = unfolded(corner_code[cyc].astype(jnp.int32)).astype(jnp.float32)
            tiles[cyc, 8 + core] = jnp.exp(value * (1.0 / CODE))

            @pl.when(core == 1)
            def _():
                far4_copy(cyc, 1).wait_recv()
                decode(2)

        @pl.when(chip + 4 >= chips)
        def _():
            clear(2)
            clear(3)

        blocks(cyc, 2, LAG // 128)

    def blocks(cyc, start, stop):
        row = lax.broadcasted_iota(jnp.int32, (128, 128), 0)
        lane = lax.broadcasted_iota(jnp.int32, (128, 128), 1)
        inside = lane + row < 128

        def turned(j):
            piece = tiles[cyc, core + j]
            for bit in (1, 2, 4):
                piece = jnp.where(row // bit % 2 == 1, pltpu.roll(piece, 128 - bit, 1), piece)
            return jnp.concatenate(
                [piece[:8]] + [pltpu.roll(piece[r : r + 8], 128 - r, 1) for r in range(8, 128, 8)],
                axis=0,
            )

        now = turned(start)
        for j in range(start, stop):
            later = turned(j + 1)
            out[cyc, :, j * 128 : j * 128 + 128] = jnp.where(inside, now, later)
            now = later

    for o in range(mod_count):
        pltpu.make_async_copy(counts.at[o], counts.at[o], count_recv.at[o]).wait()
    near(0)
    near(1)

    def share(start, stop):
        @pl.loop(start, stop)
        def _(k):
            share_stage(k)

    share(0, mod_count)
    gather_far(0, 0, mod_count)
    far_tiles(0)
    split = max(1, mod_count - 2)
    share(mod_count, mod_count + split)
    gather_far(1, 0, split)
    share(mod_count + split, steps)
    gather_far(1, split, mod_count)
    far_tiles(1)
    finish(0)
    finish(1)

    def sent(lane, slot):
        pltpu.make_async_copy(held.at[slot], held.at[slot], send_sem.at[lane]).wait()

    def sent_half(lane, slot):
        part = held.at[slot, pl.ds(0, mod_count)]
        pltpu.make_async_copy(part, part, send_sem.at[lane]).wait()

    @pl.when(first | last)
    def _():
        sent_half(8, up1)
        sent_half(9, up2)

    for cyc in range(2):
        part = held.at[own, pl.ds(cyc * mod_count + 1, mod_count - 1)]
        pltpu.make_async_copy(part, part, send_sem.at[0]).wait()
    for o in range(1, mod_count):
        pltpu.make_async_copy(counts.at[o], counts.at[o], count_send.at[o]).wait()
    for lane, slot, cond in (
        (1, own, has_dn1), (2, own, has_up1), (3, own, None), (4, down1, has_up1 & has_dn1),
        (5, down1, has_up1), (6, up1, has_up1 & has_dn1), (7, down2, has_up2),
    ):
        if cond is None:
            sent(lane, slot)
        else:
            pl.when(cond)(functools.partial(sent, lane, slot))
    for cyc in range(2):
        @pl.when(sends3)
        def _():
            far3_copy(cyc).wait_send()

        @pl.when(sends4)
        def _():
            far4_copy(cyc, 0).wait_send()

            @pl.when(core == 1)
            def _():
                far4_copy(cyc, 1).wait_send()


def shards(frames, cycle_label, good_pixel):
    frame_count, mod_count = lax.axis_size("frame"), lax.axis_size("mod")
    rows, pixels = frames.shape
    steps = 2 * mod_count
    per_cycle = pixels // steps
    small = (pixels // 128, 128)
    return pl.pallas_call(
        functools.partial(kernel, frame_count, mod_count),
        out_shape=jax.ShapeDtypeStruct((2, rows, LAG), jnp.float32),
        in_specs=[pl.BlockSpec(memory_space=pl.ANY)] * 3,
        out_specs=pl.BlockSpec(memory_space=pltpu.VMEM),
        scratch_shapes=[
            pltpu.VMEM((rows, pixels), jnp.bfloat16),
            pltpu.VMEM(small, jnp.int32),
            pltpu.VMEM(small, jnp.int32),
            pltpu.VMEM((pixels, 128), jnp.float32),
            pltpu.VMEM((mod_count, 8, 128), jnp.float32),
            pltpu.VMEM((steps, rows, per_cycle), jnp.bfloat16),
            pltpu.VMEM((10, steps, rows, per_cycle), jnp.bfloat16),
            pltpu.VMEM((mod_count, 8, 128), jnp.float32),
            pltpu.VMEM((2, 10, 128, 128), jnp.float32),
            pltpu.VMEM((2, 3, 128, 128), jnp.int16),
            pltpu.VMEM((2, 3, 128, 128), jnp.int16),
            pltpu.VMEM((2, 80, 128), jnp.int16),
            pltpu.VMEM((2, 80, 128), jnp.int16),
            pltpu.VMEM((3 * rows + 16, 256), jnp.float32),
            pltpu.VMEM((2, 3, 128, 128), jnp.float32),
            pltpu.SemaphoreType.DMA((3,)),
            pltpu.SemaphoreType.DMA((10, steps)),
            pltpu.SemaphoreType.DMA((10,)),
            pltpu.SemaphoreType.DMA((mod_count,)),
            pltpu.SemaphoreType.DMA((mod_count,)),
            pltpu.SemaphoreType.DMA((2, 3)),
            pltpu.SemaphoreType.DMA((2, 3)),
        ],
        compiler_params=pltpu.CompilerParams(
            collective_id=0, has_side_effects=True, vmem_limit_bytes=32 * 1024 * 1024
        ),
    )(pltpu.with_memory_space_constraint(frames, pltpu.HBM), cycle_label.reshape(small), good_pixel.reshape(small))


def solution(mesh):
    placed = (P("frame", "mod"), P("mod"), P("mod"))
    return jax.shard_map(
        shards, mesh=mesh, in_specs=placed, out_specs=P("mod", "frame", None), check_vma=False
    )
```

```python
import functools

import jax
import jax.numpy as jnp
from jax import lax
from jax.experimental import pallas as pl
from jax.experimental.pallas import tpu as pltpu
from jax.sharding import PartitionSpec as P

CYCLES = 16
LAG = 1024
MESH = pl.DeviceIdType.MESH
TRANSIT_LAG = 2
OWN_LAG = 5
RELAY_LAG = 6
CODE = 5600.0
NT = (((1,), (1,)), ((), ()))


def nt_dot(a, b):
    return lax.dot_general(a, b, NT, preferred_element_type=jnp.float32)


def rank_pixels(label_ref, good_ref, place, partial, cycles, per_cycle):
    rows, lanes = label_ref.shape
    label = label_ref[...]
    good = good_ref[...] > 0
    member = jnp.concatenate([jnp.where(label == c, 1.0, 0.0) for c in range(cycles)], axis=0)
    before = lax.broadcasted_iota(jnp.int32, (lanes, lanes), 0)
    at = lax.broadcasted_iota(jnp.int32, (lanes, lanes), 1)
    upper = jnp.where(before < at, 1.0, 0.0).astype(jnp.bfloat16)
    ones = jnp.ones((lanes, lanes), jnp.bfloat16)
    packed = member.astype(jnp.bfloat16)
    in_row = jnp.dot(packed, upper, preferred_element_type=jnp.float32)
    totals = jnp.dot(packed, ones, preferred_element_type=jnp.float32).astype(jnp.bfloat16)
    side = jnp.concatenate([totals[c * rows : (c + 1) * rows] for c in range(cycles)], axis=1)
    here = lax.broadcasted_iota(jnp.int32, (rows, rows), 0)
    there = lax.broadcasted_iota(jnp.int32, (rows, rows), 1)
    earlier = jnp.where(there < here, 1.0, 0.0).astype(jnp.bfloat16)
    above = jnp.dot(earlier, side, preferred_element_type=jnp.float32)
    usable = jnp.where(good, 1.0, 0.0)
    partial[...] = jnp.zeros_like(partial)
    total = None
    for c in range(cycles):
        mine = slice(c * rows, (c + 1) * rows)
        ranks = (in_row[mine] + above[:, c * lanes : (c + 1) * lanes]) * member[mine]
        total = ranks if total is None else total + ranks
        per_row = jnp.sum(member[mine] * usable, axis=0, keepdims=True)
        partial[c // 2, c % 2 : c % 2 + 1, :] = jnp.broadcast_to(
            jnp.sum(per_row, axis=1, keepdims=True), (1, lanes)
        )
    where = jnp.where(good, total + label.astype(jnp.float32) * per_cycle, -1.0)
    for r in range(rows):
        place[r * lanes : (r + 1) * lanes, :] = jnp.broadcast_to(where[r : r + 1], (lanes, lanes)).T


def kernel(
    frame_count, mod_count, frames_hbm, label_hbm, good_hbm, out,
    frames, label, good, place, partial, packed, held, counts, tiles, far, code, corner, corner_code, gram, sums,
    in_sem, recv_sem, send_sem, count_send, count_recv, far_send, far_recv,
):
    f = lax.axis_index("frame")
    m = lax.axis_index("mod")
    core = f % 2
    chip = f // 2
    chips = frame_count // 2
    y_count = mod_count // 2
    y, x = m // 2, m % 2
    partner = f + 1 - 2 * core
    steps = 2 * mod_count
    cycles = 2 * mod_count
    rows, per_cycle = packed.shape[1:]

    has_up1, has_up2 = chip + 1 < chips, chip + 2 < chips
    has_dn1, has_dn2 = chip >= 1, chip >= 2

    own, down1, down2, up1, up2 = 4 + core, 6 + core, 8 + core, 2 + core, core
    other_down1, other_down2, other_own = 7 - core, 9 - core, 5 - core

    loads = [
        pltpu.make_async_copy(src, dst, in_sem.at[i])
        for i, (src, dst) in enumerate(
            ((label_hbm, label), (good_hbm, good), (frames_hbm, frames))
        )
    ]
    for load in loads:
        load.start()

    half = chips // 2
    first, last = chip == 0, chip == chips - 1
    below, above = chip == half - 1, chip == half
    at_first, at_last = core, frame_count - 2 + core
    at_below, at_above = 2 * half - 2 + core, 2 * half + core

    def peer(o, sign):
        dy, dx = o // 2, o % 2
        return ((y + sign * dy + y_count) % y_count) * 2 + (x + dx) % 2

    barrier = pltpu.get_barrier_semaphore()

    def greet(cond, fr, mo):
        @pl.when(cond)
        def _():
            pl.semaphore_signal(barrier, inc=1, device_id=(fr, mo), device_id_type=MESH)

    for o in range(1, mod_count):
        pl.semaphore_signal(barrier, inc=1, device_id=(f, peer(o, 1)), device_id_type=MESH)
    pl.semaphore_signal(barrier, inc=1, device_id=(partner, m), device_id_type=MESH)
    greet(has_up1, f + 2, m)
    greet(has_up2, f + 4, m)
    greet(has_dn1, f - 2, m)
    greet(has_dn2, f - 4, m)
    for ends, targets in (
        (first | last, (at_below, at_above)), (below | above, (at_first, at_last))
    ):
        for target in targets:
            greet(ends, target, m)
    arrivals = mod_count
    ends = first | last | below | above
    for cond in (has_up1, has_up2, has_dn1, has_dn2, ends, ends):
        arrivals = arrivals + jnp.where(cond, 1, 0)

    loads[0].wait()
    loads[1].wait()
    rank_pixels(label, good, place, partial, cycles, per_cycle)
    loads[2].wait()
    pl.semaphore_wait(barrier, arrivals)

    def remote(src, dst, send, recv, fr, mo):
        return pltpu.make_async_remote_copy(
            src_ref=src, dst_ref=dst, send_sem=send, recv_sem=recv,
            device_id=(fr, mo), device_id_type=MESH,
        )

    def forward(from_slot, to_slot, k, lane, fr):
        source = packed.at[k] if from_slot is None else held.at[from_slot, k]
        remote(
            source, held.at[to_slot, k], send_sem.at[lane],
            recv_sem.at[to_slot, k], fr, m,
        ).start()

    def arrived(slot, k):
        pltpu.make_async_copy(held.at[slot, k], held.at[slot, k], recv_sem.at[slot, k]).wait()

    def arrange(k):
        cyc, o = k // mod_count, k % mod_count
        cycle = 2 * peer(o, -1) + cyc
        lane = lax.broadcasted_iota(jnp.int32, (256, 128), 1) + cycle * per_cycle
        wanted = [(lane + h * 128).astype(jnp.float32) for h in range(per_cycle // 128)]
        total = None
        for r in range(0, frames.shape[1], 256):
            spot = place[r : r + 256, :]
            hot = jnp.concatenate(
                [jnp.where(spot == w, 1.0, 0.0).astype(jnp.bfloat16) for w in wanted], axis=1
            )
            term = jnp.dot(frames[:, r : r + 256], hot, preferred_element_type=jnp.float32)
            total = term if total is None else total + term
        packed[k] = total.astype(jnp.bfloat16)

    def launch(k):
        o = k % mod_count

        @pl.when(o == 0)
        def _():
            pltpu.make_async_copy(packed.at[k], held.at[own, k], recv_sem.at[own, k]).start()

        @pl.when(o > 0)
        def _():
            remote(
                packed.at[k], held.at[own, k], send_sem.at[0], recv_sem.at[own, k], f, peer(o, -1)
            ).start()

    def forward_down(from_slot, to_slot, by_slot, k, lane):
        detour = above & (k % 2 == 1)

        @pl.when(detour)
        def _():
            forward(from_slot, by_slot, k, lane, at_first)

        @pl.when(has_dn1 & jnp.logical_not(detour))
        def _():
            forward(from_slot, to_slot, k, lane, f - 2)

    def forward_up(from_slot, to_slot, by_slot, k, lane):
        detour = below & (k % 2 == 1)

        @pl.when(detour)
        def _():
            forward(from_slot, by_slot, k, lane, at_last)

        @pl.when(has_up1 & jnp.logical_not(detour))
        def _():
            forward(from_slot, to_slot, k, lane, f + 2)

    def transit(up_slot, down_slot, k, lane):
        @pl.when(first)
        def _():
            arrived(up_slot, k)
            forward(up_slot, down_slot, k, lane, at_below)

        @pl.when(last)
        def _():
            arrived(down_slot, k)
            forward(down_slot, up_slot, k, lane, at_above)

    def own_stage(k, source):
        forward_down(source, down1, up1, k, 1)
        forward_up(source, up1, down1, k, 2)
        forward(source, own, k, 3, partner)

    def relay_stage(k):
        @pl.when(has_up1)
        def _():
            arrived(down1, k)
            forward_down(down1, down2, up2, k, 4)
            forward(down1, down1, k, 5, partner)

        @pl.when(has_dn1)
        def _():
            arrived(up1, k)
            forward_up(up1, up2, down2, k, 6)

    def share_stage(k):
        @pl.when(has_up2)
        def _():
            arrived(down2, k)
            forward(down2, down2, k, 7, partner)

    for o in range(mod_count):
        to = peer(o, -1)
        if o == 0:
            pltpu.make_async_copy(partial.at[to], counts.at[o], count_recv.at[o]).start()
        else:
            remote(partial.at[to], counts.at[o], count_send.at[o], count_recv.at[o], f, to).start()

    def slab(i):
        early = jnp.where(i == 1, mod_count, i - 1)
        return jnp.where((i >= 1) & (i <= mod_count), early, i)

    @pl.loop(0, steps + OWN_LAG + RELAY_LAG + TRANSIT_LAG)
    def _(i):
        @pl.when(i < steps)
        def _():
            arrange(slab(i))

        @pl.when((i >= 1) & (i <= steps))
        def _():
            launch(slab(i - 1))

        @pl.when((i >= 1) & (i < 3))
        def _():
            own_stage(slab(i - 1), None)

        @pl.when((i >= OWN_LAG + 2) & (i < steps + OWN_LAG))
        def _():
            arrived(own, slab(i - OWN_LAG))
            own_stage(slab(i - OWN_LAG), own)

        passed = slab(i - OWN_LAG - TRANSIT_LAG)

        @pl.when((i >= OWN_LAG + TRANSIT_LAG) & (passed < steps) & (passed % 2 == 1))
        def _():
            transit(up1, down1, passed, 8)

        relayed = i - OWN_LAG - RELAY_LAG

        @pl.when((relayed >= 0) & (relayed < steps))
        def _():
            relay_stage(slab(relayed))

        passed_on = slab(relayed - TRANSIT_LAG)

        @pl.when((relayed >= TRANSIT_LAG) & (passed_on % 2 == 1))
        def _():
            transit(up2, down2, passed_on, 9)

    def far3_copy(cyc):
        return remote(
            far.at[cyc, pl.ds(0, 2)], code.at[cyc, pl.ds(0, 2)],
            far_send.at[cyc, 0], far_recv.at[cyc, 0], f - 2, m,
        )

    def far4_copy(cyc, i):
        source, target = (far, code) if i else (corner, corner_code)
        place_of = (cyc, 2) if i else (cyc,)
        return remote(
            source.at[place_of], target.at[place_of],
            far_send.at[cyc, 1 + i], far_recv.at[cyc, 1 + i], f - 4, m,
        )

    def folded(tile):
        lane = lax.broadcasted_iota(jnp.int32, (8, 128), 1)
        parts = [
            jnp.where(
                lane < 8 * g + 8,
                tile[8 * g : 8 * g + 8],
                pltpu.roll(tile[112 - 8 * g : 120 - 8 * g], 8 * g + 8, 1),
            )
            for g in range(8, 15)
        ]
        return jnp.concatenate(parts + [tile[120:], tile[56:64], tile[56:64]], axis=0)

    def unfolded(tile):
        parts = [
            pltpu.roll(tile[8 * (6 - h) : 8 * (6 - h) + 8], 8 * h + 8, 1) for h in range(7)
        ]
        return jnp.concatenate(parts + [tile[64:72], tile[:56], tile[56:64]], axis=0)

    sends3, sends4 = has_dn1 & has_up2, has_dn2 & has_up2

    everything = range(mod_count)

    def products(cyc, lhs_slots, rhs_slot, span):
        ones = jnp.ones((16, per_cycle), jnp.bfloat16)
        total = None
        for o in span:
            k = cyc * mod_count + o
            lhs = jnp.concatenate([held[s, k] for s in lhs_slots] + [ones], axis=0)
            rhs = held[rhs_slot : rhs_slot + 2, k].reshape(2 * rows, per_cycle)
            term = nt_dot(lhs, rhs)
            total = term if total is None else total + term
        return total

    def row_sums(cyc, slot, span):
        total = None
        for o in span:
            block = held[slot, cyc * mod_count + o].astype(jnp.float32)
            total = block if total is None else total + block
        return jnp.broadcast_to(jnp.sum(total, axis=1, keepdims=True), (rows, 128))

    def cycle_count(cyc):
        count = counts[0]
        for o in range(1, mod_count):
            count = count + counts[o]
        return count[cyc : cyc + 1]

    def correlated(total, i, earlier, later, side, count):
        span = slice(side * 128, side * 128 + 128)
        return total[i * 128 : i * 128 + 128, span] * count / (earlier * later[:, span])

    def near(cyc):
        @pl.loop(0, mod_count)
        def _(o):
            k = cyc * mod_count + o
            arrived(other_own, k)

            @pl.when(has_up1)
            def _():
                arrived(other_down1, k)

        arrived(own, cyc * mod_count)
        count = cycle_count(cyc)
        mine = row_sums(cyc, own, everything)
        sums[cyc, 0] = mine

        @pl.when(has_dn1)
        def _():
            sums[cyc, 1] = row_sums(cyc, up1, everything)

        def part(rhs_slot):
            total = products(cyc, (own,), rhs_slot, everything)
            for side in range(2):
                tiles[cyc, rhs_slot - 4 + side] = correlated(
                    total, 0, mine, total[rows : rows + 1], side, count
                )

        part(4)

        @pl.when(has_up1)
        def _():
            part(6)

        @pl.when(jnp.logical_not(has_up1))
        def _():
            tiles[cyc, 2:4] = jnp.zeros((2, 128, 128), jnp.float32)

        blocks(cyc, 0, 2)

    def gather_far(cyc, start, stop):
        @pl.loop(start, stop)
        def _(o):
            k = cyc * mod_count + o

            @pl.when(has_up2)
            def _():
                arrived(other_down2, k)

            @pl.when(has_dn2)
            def _():
                arrived(up2, k)

        @pl.when(has_up2)
        def _():
            span = range(start, stop)
            total = products(cyc, (up1, up2, own), 8, span)
            second = row_sums(cyc, up2, span)
            if start > 0:
                total, second = total + gram[...], second + sums[cyc, 2]
            gram[...] = total
            sums[cyc, 2] = second

    def far_tiles(cyc):
        @pl.when(has_up2)
        def _():
            count = cycle_count(cyc)
            total = gram[...]
            later = total[3 * rows : 3 * rows + 1]

            def coded(i, side):
                value = correlated(total, i, sums[cyc, 1 + i], later, side, count)
                return jnp.round(jnp.log(value) * CODE).astype(jnp.int32)

            near_side, far_side = coded(1, 0), coded(1, 1)
            far[cyc, 2] = near_side.astype(jnp.int16)
            corner[cyc] = folded(jnp.where(core == 0, near_side, far_side)).astype(jnp.int16)
            for side in range(2):
                far[cyc, side] = coded(0, side).astype(jnp.int16)
            for side in range(2):
                tiles[cyc, 4 + side] = correlated(total, 2, sums[cyc, 0], later, side, count)

        @pl.when(sends4)
        def _():
            far4_copy(cyc, 0).start()

            @pl.when(core == 1)
            def _():
                far4_copy(cyc, 1).start()

        @pl.when(sends3)
        def _():
            far3_copy(cyc).start()

        @pl.when(jnp.logical_not(has_up2))
        def _():
            tiles[cyc, 4:6] = jnp.zeros((2, 128, 128), jnp.float32)

    def finish(cyc):
        def decode(i):
            value = code[cyc, i].astype(jnp.int32).astype(jnp.float32)
            tiles[cyc, 6 + i] = jnp.exp(value * (1.0 / CODE))

        def clear(i):
            tiles[cyc, 6 + i] = jnp.zeros((128, 128), jnp.float32)

        @pl.when(chip + 3 < chips)
        def _():
            far3_copy(cyc).wait_recv()
            decode(0)
            decode(1)

        @pl.when(chip + 3 >= chips)
        def _():
            clear(0)
            clear(1)

        @pl.when(chip + 4 < chips)
        def _():
            far4_copy(cyc, 0).wait_recv()
            value = unfolded(corner_code[cyc].astype(jnp.int32)).astype(jnp.float32)
            tiles[cyc, 8 + core] = jnp.exp(value * (1.0 / CODE))

            @pl.when(core == 1)
            def _():
                far4_copy(cyc, 1).wait_recv()
                decode(2)

        @pl.when(chip + 4 >= chips)
        def _():
            clear(2)
            clear(3)

        blocks(cyc, 2, LAG // 128)

    def blocks(cyc, start, stop):
        row = lax.broadcasted_iota(jnp.int32, (128, 128), 0)
        lane = lax.broadcasted_iota(jnp.int32, (128, 128), 1)
        inside = lane + row < 128

        def turned(j):
            piece = tiles[cyc, core + j]
            for bit in (1, 2, 4):
                piece = jnp.where(row // bit % 2 == 1, pltpu.roll(piece, 128 - bit, 1), piece)
            return jnp.concatenate(
                [piece[:8]] + [pltpu.roll(piece[r : r + 8], 128 - r, 1) for r in range(8, 128, 8)],
                axis=0,
            )

        now = turned(start)
        for j in range(start, stop):
            later = turned(j + 1)
            out[cyc, :, j * 128 : j * 128 + 128] = jnp.where(inside, now, later)
            now = later

    for o in range(mod_count):
        pltpu.make_async_copy(counts.at[o], counts.at[o], count_recv.at[o]).wait()
    near(0)
    near(1)

    def share(start, stop):
        @pl.loop(start, stop)
        def _(k):
            share_stage(k)

    share(0, mod_count)
    gather_far(0, 0, mod_count)
    far_tiles(0)
    split = max(1, mod_count - 2)
    share(mod_count, mod_count + split)
    gather_far(1, 0, split)
    share(mod_count + split, steps)
    gather_far(1, split, mod_count)
    far_tiles(1)
    finish(0)
    finish(1)

    def sent(lane, slot):
        pltpu.make_async_copy(held.at[slot], held.at[slot], send_sem.at[lane]).wait()

    def sent_half(lane, slot):
        part = held.at[slot, pl.ds(0, mod_count)]
        pltpu.make_async_copy(part, part, send_sem.at[lane]).wait()

    @pl.when(first | last)
    def _():
        sent_half(8, up1)
        sent_half(9, up2)

    for cyc in range(2):
        part = held.at[own, pl.ds(cyc * mod_count + 1, mod_count - 1)]
        pltpu.make_async_copy(part, part, send_sem.at[0]).wait()
    for o in range(1, mod_count):
        pltpu.make_async_copy(counts.at[o], counts.at[o], count_send.at[o]).wait()
    for lane, slot, cond in (
        (1, own, has_dn1), (2, own, has_up1), (3, own, None), (4, down1, has_up1 & has_dn1),
        (5, down1, has_up1), (6, up1, has_up1 & has_dn1), (7, down2, has_up2),
    ):
        if cond is None:
            sent(lane, slot)
        else:
            pl.when(cond)(functools.partial(sent, lane, slot))
    for cyc in range(2):
        @pl.when(sends3)
        def _():
            far3_copy(cyc).wait_send()

        @pl.when(sends4)
        def _():
            far4_copy(cyc, 0).wait_send()

            @pl.when(core == 1)
            def _():
                far4_copy(cyc, 1).wait_send()


def shards(frames, cycle_label, good_pixel):
    frame_count, mod_count = lax.axis_size("frame"), lax.axis_size("mod")
    rows, pixels = frames.shape
    steps = 2 * mod_count
    per_cycle = pixels // steps
    small = (pixels // 128, 128)
    return pl.pallas_call(
        functools.partial(kernel, frame_count, mod_count),
        out_shape=jax.ShapeDtypeStruct((2, rows, LAG), jnp.float32),
        in_specs=[pl.BlockSpec(memory_space=pl.ANY)] * 3,
        out_specs=pl.BlockSpec(memory_space=pltpu.VMEM),
        scratch_shapes=[
            pltpu.VMEM((rows, pixels), jnp.bfloat16),
            pltpu.VMEM(small, jnp.int32),
            pltpu.VMEM(small, jnp.int32),
            pltpu.VMEM((pixels, 128), jnp.float32),
            pltpu.VMEM((mod_count, 8, 128), jnp.float32),
            pltpu.VMEM((steps, rows, per_cycle), jnp.bfloat16),
            pltpu.VMEM((10, steps, rows, per_cycle), jnp.bfloat16),
            pltpu.VMEM((mod_count, 8, 128), jnp.float32),
            pltpu.VMEM((2, 10, 128, 128), jnp.float32),
            pltpu.VMEM((2, 3, 128, 128), jnp.int16),
            pltpu.VMEM((2, 3, 128, 128), jnp.int16),
            pltpu.VMEM((2, 80, 128), jnp.int16),
            pltpu.VMEM((2, 80, 128), jnp.int16),
            pltpu.VMEM((3 * rows + 16, 256), jnp.float32),
            pltpu.VMEM((2, 3, 128, 128), jnp.float32),
            pltpu.SemaphoreType.DMA((3,)),
            pltpu.SemaphoreType.DMA((10, steps)),
            pltpu.SemaphoreType.DMA((10,)),
            pltpu.SemaphoreType.DMA((mod_count,)),
            pltpu.SemaphoreType.DMA((mod_count,)),
            pltpu.SemaphoreType.DMA((2, 3)),
            pltpu.SemaphoreType.DMA((2, 3)),
        ],
        compiler_params=pltpu.CompilerParams(
            collective_id=0, has_side_effects=True, vmem_limit_bytes=32 * 1024 * 1024
        ),
    )(pltpu.with_memory_space_constraint(frames, pltpu.HBM), cycle_label.reshape(small), good_pixel.reshape(small))


def solution(mesh):
    placed = (P("frame", "mod"), P("mod"), P("mod"))
    return jax.shard_map(
        shards, mesh=mesh, in_specs=placed, out_specs=P("mod", "frame", None), check_vma=False
    )
```
